32 devices in a mesh: grp: 2 (over y), gx: 4 (over z), gy: 2 (over x), gz: 2 (over core).
Axes of the slice: x: 2, y: 2, z: 4, core: 2. Of those that a mesh axis runs over, the one named last changes fastest.
Arguments:
- snapshot: bfloat16 [2048, 4, 16, 1024], P(('grp', 'gx'), None, 'gz', 'gy'), parts along dimension 0, may hold values from -16 to 16
- x_basis: bfloat16 [2048, 128], P('grp'), parts along dimension 0, may hold values from -0.1875 to 0.1875
- y_basis: bfloat16 [2048, 128], P('grp'), parts along dimension 0, may hold values from -0.1875 to 0.1875
Outputs:
- gram_out: float32 [2048, 1024], P(('grp', 'gx'), ('gy', 'gz')), parts along dimension 0
- core_out: float32 [256, 4, 16, 128], P(('grp', 'gx', 'gy'), None, 'gz'), parts along dimension 0
The draws below stay inside these ranges and needn't reach their ends.
There are 2 independent parts, one for each index of `grp`. The reference program is written for one: setup_inputs(seed, part) draws one part's arguments, and reference() takes and returns one part's arrays. A program takes and returns all parts, laid end to end along the dimension named above; each array names one. Nothing has to cross between parts.
All inputs are finite; a program needn't handle non-finite values.
Results may differ from the reference program's by a relative error of at most 0.0029.
Values may be sent and summed in bfloat16 or wider, within the bound.
No kernel may reach another device: no remote copies, remote signals or barrier semaphores. Data moves between devices by JAX's collectives and lax.ppermute only.
A program may use at most 128 MiB of HBM per device.

```python
import jax
import jax.numpy as jnp
from jax import lax

NX = 1024
NY = 1024
NC = 4
RX = 128
RY = 128
NZ = 16


def draw_snapshot(key, part):
    keys = jax.random.split(key, 4)
    noise = jax.random.normal(keys[0], (NX, NC, NZ, NY), jnp.float32)
    gains = jax.random.uniform(keys[1], (NX, 1, 1, 1), jnp.float32, 0.5, 1.5)
    shared = jax.random.normal(keys[2], (1, NC, NZ, NY), jnp.float32)
    amplitude = jax.random.uniform(keys[3], (NX, 1, 1, 1), jnp.float32, -1.0, 1.0)
    mixed = noise + 0.6 * jnp.roll(noise, 1, 0) + 0.4 * jnp.roll(noise, -1, 0)
    values = gains * mixed + amplitude * shared
    return jnp.clip(values, -16.0, 16.0).astype(jnp.bfloat16)


def centred(own_key, extent, deviation, reach, held_as=jnp.bfloat16):
    values = deviation * jax.random.normal(own_key, extent, jnp.float32)
    return jnp.clip(values, min=-reach, max=reach).astype(held_as)


def setup_inputs(seed: int = 0, part: int = 0) -> dict:
    seeds = jax.random.split(jax.random.key(seed), 4)
    part_splits = jax.random.split(jax.random.fold_in(seeds[3], part), 4)
    snapshot = draw_snapshot(jax.random.fold_in(jax.random.fold_in(seeds[3], part), 71), part)
    x_basis = centred(part_splits[1], (NX, RX), NX ** -0.5, 0.1875)
    y_basis = centred(part_splits[2], (NY, RY), NY ** -0.5, 0.1875)
    return {"snapshot": snapshot, "x_basis": x_basis, "y_basis": y_basis}


def reference(snapshot, x_basis, y_basis):
    unfold = snapshot.reshape(NX, NC * NZ * NY)
    inverse = 1.0 / (NC * NZ * NY)
    gram_out = jnp.dot(unfold, unfold.T, preferred_element_type=jnp.float32) * inverse
    projected = lax.dot_general(x_basis, unfold, (((0,), (0,)), ((), ())), preferred_element_type=jnp.float32).astype(jnp.bfloat16)
    core_out = jnp.dot(projected.reshape(RX * NC * NZ, NY), y_basis, preferred_element_type=jnp.float32)
    return gram_out, core_out.reshape(RX, NC, NZ, RY)
```

```python
import jax
import jax.numpy as jnp
from jax import lax
from jax.sharding import PartitionSpec as P

F32 = jnp.float32
BF16 = jnp.bfloat16
NEAR = [(0, 1), (3, 2)]
CROSS = [(1, 2), (2, 1)]
FAR = [(0, 2), (3, 1)]
NEAR_BACK = [(1, 0), (2, 3)]
FAR_BACK = [(1, 3), (2, 0)]
SWAP = [(0, 1), (1, 0)]


def gathered(snapshot, x_basis, y_basis):
    rows_local = snapshot.shape[0]
    columns = snapshot.shape[1] * snapshot.shape[2] * snapshot.shape[3]
    unfolded = snapshot.reshape(rows_local, columns)
    rank_count = x_basis.shape[1]
    rank_rows = rank_count // lax.axis_size("gx")
    inverse = 1.0 / (columns * lax.axis_size("gy") * lax.axis_size("gz"))
    basis_cols = lax.dynamic_slice_in_dim(x_basis, lax.axis_index("gx") * rank_rows, rank_rows, 1)
    shard_rows = lax.all_gather(unfolded, "gx", axis=0, tiled=True)
    gram_rows = nt(unfolded, shard_rows)
    own_rows = tn(basis_cols, shard_rows).astype(BF16)
    gram_out = lax.psum_scatter(gram_rows * inverse, ("gy", "gz"), scatter_dimension=1, tiled=True)
    shaped = own_rows.reshape(rank_rows, *snapshot.shape[1:])
    along_y = lax.all_to_all(shaped, "gy", split_axis=0, concat_axis=3, tiled=True)
    core_flat = jnp.dot(along_y.reshape(-1, along_y.shape[3]), y_basis, preferred_element_type=F32)
    return gram_out, core_flat.reshape(*along_y.shape[:3], y_basis.shape[1])


def nt(a, b):
    return lax.dot_general(a, b, (((1,), (1,)), ((), ())), preferred_element_type=F32)


def tn(a, b):
    return lax.dot_general(a, b, (((0,), (0,)), ((), ())), preferred_element_type=F32)


def meeting(snapshot, x_basis, y_basis):
    rows, ncomp, nz, ny = snapshot.shape
    rank = x_basis.shape[1]
    gx, gy, gz = lax.axis_index("gx"), lax.axis_index("gy"), lax.axis_index("gz")
    side = gx // 2
    inner = (gx == 1) | (gx == 2)
    half = ncomp // 2
    width = nz * ny
    inverse = 1.0 / (ncomp * width * lax.axis_size("gy") * lax.axis_size("gz"))

    def take(start):
        return lax.dynamic_slice_in_dim(snapshot, start, 1, 1).reshape(rows, nz, ny)

    own_raw = [take((1 - side) * half + h) for h in range(half)]
    oth_raw = [take(side * half + h) for h in range(half)]
    near_raw, cross_raw = [], []
    for h in range(half):
        near_raw.append(lax.ppermute(own_raw[h], "gx", NEAR))
        cross_raw.append(lax.ppermute(oth_raw[h], "gx", CROSS))

    def flat(a):
        return a.reshape(rows, width)

    oth = [flat(a) for a in oth_raw]
    own = [flat(a) for a in own_raw]
    cuts = [(0, 0, 8), (1, 0, 6), (1, 6, 8)]
    far = []
    for h, lo, hi in cuts:
        far.append(lax.ppermute(oth[h][:, lo * ny : hi * ny], "gx", FAR))
    near = [flat(a) for a in near_raw]
    cross = [flat(a) for a in cross_raw]

    n_at = jnp.where(side == 0, 0, 3)
    c_at = jnp.where(side == 0, 2, 1)
    f_at = jnp.where(side == 0, 3, 0)

    def basis(at):
        return lax.dynamic_slice_in_dim(x_basis, at * rows, rows, 0)

    b_n, b_s, b_c, b_f = basis(n_at), basis(gx), basis(c_at), basis(f_at)

    def total(f, *lists):
        return sum(f(*items) for items in zip(*lists))

    diag = total(lambda a: nt(a, a), own) + total(lambda a: nt(a, a), oth)
    ns = total(nt, near, own)
    sn = total(nt, own, near)
    nc_ = total(nt, near, cross)
    cn = total(nt, cross, near)
    sc = total(nt, own, cross)
    cs = total(nt, cross, own)
    zero = jnp.zeros_like(diag)
    row_n = [zero, ns, nc_, zero]
    row_s = [sn + jnp.where(inner, zero, diag), jnp.where(inner, diag, zero), sc, zero]
    row_c = [cn, cs, zero, zero]

    def placed(blocks):
        return jnp.concatenate(
            [jnp.where(side == 0, blocks[k], blocks[3 - k]) for k in range(4)], 1
        )

    early = jnp.concatenate([placed(row_n), placed(row_s), placed(row_c)], 0)
    early = lax.psum_scatter(early, ("gy", "gz"), scatter_dimension=1, tiled=True)
    gram = (
        early[rows : 2 * rows]
        + lax.ppermute(early[:rows], "gx", NEAR_BACK)
        + lax.ppermute(early[2 * rows :], "gx", CROSS)
    )

    part = [
        tn(b_n, near[h]) + tn(b_s, own[h]) + tn(b_c, cross[h]) for h in range(half)
    ]
    y_own = lax.dynamic_slice_in_dim(y_basis, gy * ny, ny, 0)
    own_out, oth_out = [], []
    fs, fc, fn = zero, zero, zero
    for (h, lo, hi), f in zip(cuts, far):
        span = slice(lo * ny, hi * ny)
        fn = fn + nt(f, near[h][:, span])
        fs = fs + nt(f, own[h][:, span])
        fc = fc + nt(f, cross[h][:, span])
        projected = (part[h][:, span] + tn(b_f, f)).astype(BF16)
        cz = hi - lo
        core = jnp.dot(projected.reshape(rank * cz, ny), y_own, preferred_element_type=F32)
        core = core.reshape(4, 2, rank // 8, cz, -1)
        keep = lax.dynamic_index_in_dim(core, gy, 1, False)
        give = lax.dynamic_index_in_dim(core, 1 - gy, 1, False)
        summed = keep + lax.ppermute(give, "gy", SWAP)

        def block(at):
            return lax.dynamic_index_in_dim(summed, at, 0, False)

        own_out.append(
            lax.ppermute(block(n_at), "gx", NEAR_BACK)
            + jnp.where(inner, block(gx), 0.0)
        )
        oth_out.append(
            lax.ppermute(block(c_at), "gx", CROSS) + lax.ppermute(block(f_at), "gx", FAR_BACK)
        )
    late = placed([fn, fs, fc, zero]).reshape(rows, 2, 2, rows)
    mine = lax.dynamic_index_in_dim(late, gz, 2, False)
    give = lax.dynamic_index_in_dim(late, 1 - gz, 2, False)
    late = mine + lax.ppermute(give, "gz", SWAP)
    mine = lax.dynamic_index_in_dim(late, gy, 1, False)
    give = lax.dynamic_index_in_dim(late, 1 - gy, 1, False)
    late = mine + lax.ppermute(give, "gy", SWAP)
    turn = [(4 + l, 4 * l + 3) for l in (0, 1, 2)] + [(8 + l, 4 * l) for l in (1, 2, 3)]
    gram = (
        gram
        + lax.ppermute(late, "gx", FAR_BACK)
        + lax.ppermute(late, ("gx", "gy", "gz"), turn).T
    )
    own_half = jnp.concatenate(own_out, 1)
    oth_half = jnp.concatenate(oth_out, 1)
    low = jnp.where(side == 0, oth_half, own_half)
    high = jnp.where(side == 0, own_half, oth_half)
    core_out = jnp.concatenate([low, high], 1).reshape(rank // 8, ncomp, nz, -1)
    return gram * inverse, core_out


def solution(mesh):
    in_specs = (P(("grp", "gx"), None, "gz", "gy"), P("grp", None), P("grp", None))
    out_specs = (P(("grp", "gx"), ("gy", "gz")), P(("grp", "gx", "gy"), None, "gz", None))
    sizes = (mesh.shape["gx"], mesh.shape["gy"], mesh.shape["gz"])
    body = meeting if sizes == (4, 2, 2) else gathered
    return jax.shard_map(body, mesh=mesh, in_specs=in_specs, out_specs=out_specs, check_vma=False)
```

```python
import functools

import jax
import jax.numpy as jnp
from jax import lax
from jax.experimental import pallas as pl
from jax.experimental.pallas import tpu as pltpu
from jax.sharding import PartitionSpec as P

F32 = jnp.float32
BF16 = jnp.bfloat16
NEAR = [(0, 1), (3, 2)]
CROSS = [(1, 2), (2, 1)]
FAR = [(0, 2), (3, 1)]
NEAR_BACK = [(1, 0), (2, 3)]
FAR_BACK = [(1, 3), (2, 0)]
SWAP = [(0, 1), (1, 0)]
TURN = [(4 + l, 4 * l + 3) for l in (0, 1, 2)] + [(8 + l, 4 * l) for l in (1, 2, 3)]


def nt(a, b):
    return lax.dot_general(a, b, (((1,), (1,)), ((), ())), preferred_element_type=F32)


def tn(a, b):
    return lax.dot_general(a, b, (((0,), (0,)), ((), ())), preferred_element_type=F32)


def nn(a, b):
    return jnp.dot(a, b, preferred_element_type=F32)


def gathered(snapshot, x_basis, y_basis):
    rows_local = snapshot.shape[0]
    columns = snapshot.shape[1] * snapshot.shape[2] * snapshot.shape[3]
    unfolded = snapshot.reshape(rows_local, columns)
    rank_count = x_basis.shape[1]
    rank_rows = rank_count // lax.axis_size("gx")
    inverse = 1.0 / (columns * lax.axis_size("gy") * lax.axis_size("gz"))
    basis_cols = lax.dynamic_slice_in_dim(x_basis, lax.axis_index("gx") * rank_rows, rank_rows, 1)
    shard_rows = lax.all_gather(unfolded, "gx", axis=0, tiled=True)
    gram_rows = nt(unfolded, shard_rows)
    own_rows = tn(basis_cols, shard_rows).astype(BF16)
    gram_out = lax.psum_scatter(gram_rows * inverse, ("gy", "gz"), scatter_dimension=1, tiled=True)
    shaped = own_rows.reshape(rank_rows, *snapshot.shape[1:])
    along_y = lax.all_to_all(shaped, "gy", split_axis=0, concat_axis=3, tiled=True)
    core_flat = nn(along_y.reshape(-1, along_y.shape[3]), y_basis)
    return gram_out, core_flat.reshape(*along_y.shape[:3], y_basis.shape[1])


def pairs_kernel(first, last, at, near, own, cross, other, *rest):
    if not first:
        carried, *rest = rest
    *outs, acc = rest
    step = pl.program_id(0)

    @pl.when(step == 0)
    def _():
        acc[...] = jnp.zeros_like(acc) if first else carried[...]

    n, s, c, o = near[...], own[...], cross[...], other[...]
    acc[0] += nt(n, s)
    acc[1] += nt(n, c)
    acc[2] += nt(s, c)
    acc[3] += nt(s, s) + nt(o, o)

    @pl.when(step == pl.num_programs(0) - 1)
    def _():
        if not last:
            outs[0][...] = acc[...]
            return
        gy, gz, side, inner = at[0], at[1], at[2], at[3]
        size = acc.shape[1]
        zero = jnp.zeros((size, size), F32)
        ns, nc, sc, diag = acc[0], acc[1], acc[2], acc[3]
        mid = jnp.full((size, size), inner, jnp.int32) == 1
        table = [
            [zero, ns, nc, zero],
            [ns.T + jnp.where(mid, 0.0, diag), jnp.where(mid, diag, 0.0), sc, zero],
            [nc.T, sc.T, zero, zero],
        ]
        for k in range(4):
            l = jnp.where(side == 0, k, 3 - k)
            for out, flag in zip(outs, (0, 1)):

                @pl.when(((l & 1) ^ gz) == flag)
                def _(k=k, l=l, out=out):
                    for row in range(3):
                        out[(l >> 1) ^ gy, row * size : (row + 1) * size, :] = table[row][k]


def whole(shape):
    return pl.BlockSpec(shape, lambda j, at: (0,) * len(shape))


def call(name, kernel, at, grid, in_specs, operands, out_shapes, scratch=(), types=None):
    types = types or [F32] * len(out_shapes)
    return pl.pallas_call(
        kernel,
        out_shape=tuple(jax.ShapeDtypeStruct(o, t) for o, t in zip(out_shapes, types)),
        grid_spec=pltpu.PrefetchScalarGridSpec(
            num_scalar_prefetch=1,
            grid=(grid,),
            in_specs=in_specs,
            out_specs=tuple(whole(o) for o in out_shapes),
            scratch_shapes=scratch,
        ),
        cost_estimate=pl.CostEstimate(flops=1, transcendentals=0, bytes_accessed=1),
        compiler_params=pltpu.CompilerParams(vmem_limit_bytes=40 << 20),
        name=name,
    )(at, *operands)


def once(name, kernel, at, operands, out_shapes, types=None):
    specs = [whole(o.shape) for o in operands]
    return call(name, kernel, at, 1, specs, operands, out_shapes, types=types)


def add_split_kernel(at, keep, got, first, second):
    first[...] = keep[0] + got[0]
    second[...] = keep[1] + got[1]


def add_rows_kernel(at, keep, got, *outs):
    size = keep.shape[0] // len(outs)
    for i, out in enumerate(outs):
        out[...] = keep[i * size : (i + 1) * size] + got[i * size : (i + 1) * size]


def add_home_kernel(at, keep, got, *outs):
    for k, out in enumerate(outs):
        out[...] = (keep[k] + got[k]).astype(out.dtype)


def add_late_kernel(at, keep, got, stay, leave):
    stay[...] = keep[0] + got[0]
    leave[...] = (keep[1] + got[1]).astype(leave.dtype)


def part_kernel(at, stay, got, late, turned):
    total = stay[...] + got[...]
    late[...] = total.astype(late.dtype)
    turned[...] = total.T.astype(turned.dtype)


def final_kernel(inverse, at, gram_own, gram_near, gram_cross, late, turned, *rest):
    *groups, gram, core = rest
    side, inner = at[2], at[3]
    gram[...] = (
        (gram_own[...] + gram_near[...] + gram_cross[...])
        + (late[...].astype(F32) + turned[...].astype(F32))
    ) * inverse
    nz = core.shape[2]
    half = core.shape[1] // 2
    mid = jnp.full((core.shape[0], 128), inner, jnp.int32) == 1
    j = 0
    for near, kept, cross, far in (groups[:4], groups[4:]):
        for k in range(near.shape[1] // 128):
            span = slice(k * 128, (k + 1) * 128)
            mine = jnp.where(mid, kept[:, span], near[:, span].astype(F32))
            other = cross[:, span].astype(F32) + far[:, span].astype(F32)
            c, z = divmod(j, nz)
            core[:, half * (1 - side) + c, z, :] = mine
            core[:, half * side + c, z, :] = other
            j += 1


def pairs(at, near, own, cross, other, carried, last, ny):
    rows, width = near.shape
    first = carried is None
    acc_shape = (4, rows, rows)
    return call(
        "pairs",
        functools.partial(pairs_kernel, first, last),
        at,
        width // ny,
        [pl.BlockSpec((rows, ny), lambda j, at: (0, j))] * 4 + ([] if first else [whole(acc_shape)]),
        [near, own, cross, other] + ([] if first else [carried]),
        [(2, 3 * rows, rows)] * 2 if last else [acc_shape],
        [pltpu.VMEM(acc_shape, F32)],
    )


def meet_kernel(first, last, joined, at, far, near, own, cross, basis, y_own, *rest):
    if not first:
        carried, *rest = rest
    if joined:
        old_keep, old_give, *rest = rest
    *outs, core_keep, core_give, acc = rest
    step = pl.program_id(0)
    gy, gz, side = at[0], at[1], at[2]
    base = 0
    if joined:
        base = old_keep.shape[2]

    @pl.when(step == 0)
    def _():
        acc[...] = jnp.zeros_like(acc) if first else carried[...]
        if joined:
            core_keep[:, :, :base] = old_keep[...]
            core_give[:, :, :base] = old_give[...]

    f, n, s, c = far[...], near[...], own[...], cross[...]
    projected = nn(basis[0], n) + nn(basis[1], s) + nn(basis[2], c) + nn(basis[3], f)
    part = nn(projected.astype(BF16), y_own[...])
    acc[0] += nt(f, n)
    acc[1] += nt(f, s)
    acc[2] += nt(f, c)
    few, cols = part.shape[0] // 8, part.shape[1]
    span = pl.ds(pl.multiple_of(base + step * cols, 128), cols)
    for z in range(4):
        k = jnp.where(side == 0, z, 3 - z)
        for out, flag in ((core_keep, gy), (core_give, 1 - gy)):
            for y in range(2):

                @pl.when(flag == y)
                def _(z=z, k=k, y=y, out=out):
                    start = (2 * z + y) * few
                    out[k, :, span] = part[start : start + few]

    @pl.when(step == pl.num_programs(0) - 1)
    def _():
        if not last:
            outs[0][...] = acc[...]
            return
        for k in range(4):
            l = jnp.where(side == 0, k, 3 - k)
            for out, flag in zip(outs, (0, 1)):

                @pl.when(((l & 1) ^ gz) == flag)
                def _(k=k, l=l, out=out):
                    out[(l >> 1) ^ gy] = acc[k] if k < 3 else jnp.zeros_like(acc[0])


def meet(at, far, near, own, cross, lo, basis, y_own, carried, old, last):
    rows, width = far.shape
    ny, s_cols = y_own.shape
    rank = basis.shape[1]
    n = width // ny
    first, joined = carried is None, old is not None
    shifted = pl.BlockSpec((rows, ny), lambda j, at: (0, lo + j))
    acc_shape = (3, rows, rows)
    core_shape = (4, rank // 8, n * s_cols + (old[0].shape[2] if joined else 0))
    return call(
        "meet",
        functools.partial(meet_kernel, first, last, joined),
        at,
        n,
        [pl.BlockSpec((rows, ny), lambda j, at: (0, j)), shifted, shifted, shifted]
        + [whole(basis.shape), whole(y_own.shape)]
        + ([] if first else [whole(acc_shape)])
        + ([whole(o.shape) for o in old] if joined else []),
        [far, near, own, cross, basis, y_own]
        + ([] if first else [carried])
        + (list(old) if joined else []),
        ([(2, rows, rows)] * 2 if last else [acc_shape]) + [core_shape] * 2,
        [pltpu.VMEM(acc_shape, F32)],
    )


def meeting(snapshot, x_basis, y_basis):
    rows, ncomp, nz, ny = snapshot.shape
    rank = x_basis.shape[1]
    gx, gy, gz = lax.axis_index("gx"), lax.axis_index("gy"), lax.axis_index("gz")
    side = gx // 2
    inner = (gx == 1) | (gx == 2)
    half = ncomp // 2
    width = nz * ny
    inverse = 1.0 / (ncomp * width * lax.axis_size("gy") * lax.axis_size("gz"))
    own_at, oth_at = (1 - side) * half, side * half
    at = jnp.stack([gy, gz, side, inner.astype(jnp.int32)])

    tied = lax.optimization_barrier

    def take(source, start):
        return lax.dynamic_slice_in_dim(source, start, 1, 1).reshape(rows, nz, ny)

    def flat(a):
        return a.reshape(rows, width)

    near, cross, own, oth = ([None] * half for _ in range(4))
    oth_raw = take(snapshot, oth_at)
    source, oth_raw = tied((snapshot, oth_raw))
    own_raw = take(source, own_at)
    source, own_raw = tied((source, own_raw))
    oth_late = take(source, oth_at + 1)
    source, oth_late = tied((source, oth_late))
    oth[1], own[1] = flat(oth_late), flat(take(source, own_at + 1))
    cross_raw = lax.ppermute(oth_raw, "gx", CROSS)
    near_raw = lax.ppermute(own_raw, "gx", NEAR)
    cross[1] = lax.ppermute(oth[1], "gx", CROSS)
    near[1] = lax.ppermute(own[1], "gx", NEAR)
    oth_raw, own_raw, oth[1], own[1] = tied((oth_raw, own_raw, oth[1], own[1]))
    oth[0], own[0] = flat(oth_raw), flat(own_raw)

    places = [
        jnp.where(side == 0, 0, 3),
        gx,
        jnp.where(side == 0, 2, 1),
        jnp.where(side == 0, 3, 0),
    ]
    basis = jnp.stack([lax.dynamic_slice_in_dim(x_basis, p * rows, rows, 0).T for p in places])
    y_own = lax.dynamic_slice_in_dim(y_basis, gy * ny, ny, 0)

    cuts = [(0, 0, 8), (1, 0, 3), (1, 3, 7), (1, 7, 8)]

    def send_far(i, *gate):
        data, gate = tied((sends[i], gate))
        return lax.ppermute(data, "gx", FAR), *gate

    def meets(i, far, carried, old, last=False):
        h, lo, _ = cuts[i]
        return meet(at, far, near[h], own[h], cross[h], lo, basis, y_own, carried, old, last)

    def across(core, link):
        keep, give = core
        return once(
            "add_home",
            add_home_kernel,
            at,
            [keep, lax.ppermute(give, "gy", SWAP)],
            [keep.shape[1:]] * 4,
            [link, F32, link, link],
        )

    def send_home(near, kept, cross, far):
        return (
            lax.ppermute(near, "gx", NEAR_BACK),
            kept,
            lax.ppermute(cross, "gx", CROSS),
            lax.ppermute(far, "gx", FAR_BACK),
        )

    sends = [oth[0]] + [oth[1][:, lo * ny : hi * ny] for _, lo, hi in cuts[1:]]
    sends, cross_raw, own[0] = tied((sends, cross_raw, own[0]))
    cross[0] = flat(cross_raw)
    cross[0], near_raw = tied((cross[0], near_raw))
    near[0] = flat(near_raw)
    far0, cross[0], near[0], own[0], basis, y_own = send_far(
        0, cross[0], near[0], own[0], basis, y_own
    )
    (sums,) = pairs(at, near[0], own[0], cross[0], oth[0], None, False, ny)
    sums, cross[1] = tied((sums, cross[1]))

    far1, cross[1], near[1], sums = send_far(1, cross[1], near[1], sums)
    keep, give = pairs(at, near[1], own[1], cross[1], oth[1], sums, True, ny)

    early, leave = once(
        "add_split", add_split_kernel, at, [keep, lax.ppermute(give, "gz", SWAP)], [keep.shape[1:]] * 2
    )
    far2, far0, leave = send_far(2, far0, leave)
    far0, far1 = tied((far0, far1))
    acc, *core = meets(0, far0, None, None)
    gram_near, gram_own, gram_cross = once(
        "add_rows", add_rows_kernel, at, [early, lax.ppermute(leave, "gy", SWAP)], [(rows, rows)] * 3
    )

    far3, far1, gram_own, acc = send_far(3, far1, gram_own, acc)
    acc, *core = meets(1, far1, acc, core)
    gram_near = lax.ppermute(gram_near, "gx", NEAR_BACK)
    gram_cross = lax.ppermute(gram_cross, "gx", CROSS)
    blocks = across(core, F32)
    home = send_home(*blocks)

    far2, blocks = tied((far2, blocks))
    acc, *core = meets(2, far2, acc, None)
    far3, acc, gram_near, gram_cross, home = tied(
        (far3, acc, gram_near, gram_cross, home)
    )
    keep, give, *core = meets(3, far3, acc, core, True)
    stay, leave = once(
        "add_late",
        add_late_kernel,
        at,
        [keep, lax.ppermute(give, "gz", SWAP)],
        [(rows, rows)] * 2,
        [F32, BF16],
    )
    rest = send_home(*across(core, BF16))
    late, turned = once(
        "part",
        part_kernel,
        at,
        [stay, lax.ppermute(leave, "gy", SWAP)],
        [(rows, rows)] * 2,
        [BF16] * 2,
    )
    late = lax.ppermute(late, "gx", FAR_BACK)
    turned = lax.ppermute(turned, ("gx", "gy", "gz"), TURN)
    return once(
        "final",
        functools.partial(final_kernel, inverse),
        at,
        [gram_own, gram_near, gram_cross, late, turned, *home, *rest],
        [(rows, rows), (rank // 8, ncomp, nz, y_basis.shape[1])],
    )


def solution(mesh):
    in_specs = (P(("grp", "gx"), None, "gz", "gy"), P("grp", None), P("grp", None))
    out_specs = (P(("grp", "gx"), ("gy", "gz")), P(("grp", "gx", "gy"), None, "gz", None))
    sizes = (mesh.shape["gx"], mesh.shape["gy"], mesh.shape["gz"])
    body = meeting if sizes == (4, 2, 2) else gathered
    return jax.shard_map(body, mesh=mesh, in_specs=in_specs, out_specs=out_specs, check_vma=False)
```

```python
import functools

import jax
import jax.numpy as jnp
from jax import lax
from jax.experimental import pallas as pl
from jax.experimental.pallas import tpu as pltpu
from jax.sharding import PartitionSpec as P

F32 = jnp.float32
BF16 = jnp.bfloat16
NEAR = [(0, 1), (3, 2)]
CROSS = [(1, 2), (2, 1)]
FAR = [(0, 2), (3, 1)]
NEAR_BACK = [(1, 0), (2, 3)]
FAR_BACK = [(1, 3), (2, 0)]
SWAP = [(0, 1), (1, 0)]
TURN = [(4 + l, 4 * l + 3) for l in (0, 1, 2)] + [(8 + l, 4 * l) for l in (1, 2, 3)]


def nt(a, b):
    return lax.dot_general(a, b, (((1,), (1,)), ((), ())), preferred_element_type=F32)


def tn(a, b):
    return lax.dot_general(a, b, (((0,), (0,)), ((), ())), preferred_element_type=F32)


def nn(a, b):
    return jnp.dot(a, b, preferred_element_type=F32)


def gathered(snapshot, x_basis, y_basis):
    rows_local = snapshot.shape[0]
    columns = snapshot.shape[1] * snapshot.shape[2] * snapshot.shape[3]
    unfolded = snapshot.reshape(rows_local, columns)
    rank_count = x_basis.shape[1]
    rank_rows = rank_count // lax.axis_size("gx")
    inverse = 1.0 / (columns * lax.axis_size("gy") * lax.axis_size("gz"))
    basis_cols = lax.dynamic_slice_in_dim(x_basis, lax.axis_index("gx") * rank_rows, rank_rows, 1)
    shard_rows = lax.all_gather(unfolded, "gx", axis=0, tiled=True)
    gram_rows = nt(unfolded, shard_rows)
    own_rows = tn(basis_cols, shard_rows).astype(BF16)
    gram_out = lax.psum_scatter(gram_rows * inverse, ("gy", "gz"), scatter_dimension=1, tiled=True)
    shaped = own_rows.reshape(rank_rows, *snapshot.shape[1:])
    along_y = lax.all_to_all(shaped, "gy", split_axis=0, concat_axis=3, tiled=True)
    core_flat = nn(along_y.reshape(-1, along_y.shape[3]), y_basis)
    return gram_out, core_flat.reshape(*along_y.shape[:3], y_basis.shape[1])


def pairs_kernel(first, last, at, near, own, cross, other, *rest):
    if not first:
        carried, *rest = rest
    *outs, acc = rest
    step = pl.program_id(0)

    @pl.when(step == 0)
    def _():
        acc[...] = jnp.zeros_like(acc) if first else carried[...]

    n, s, c, o = near[...], own[...], cross[...], other[...]
    acc[0] += nt(n, s)
    acc[1] += nt(n, c)
    acc[2] += nt(s, c)
    acc[3] += nt(s, s) + nt(o, o)

    @pl.when(step == pl.num_programs(0) - 1)
    def _():
        if not last:
            outs[0][...] = acc[...]
            return
        gy, gz, side, inner = at[0], at[1], at[2], at[3]
        size = acc.shape[1]
        zero = jnp.zeros((size, size), F32)
        ns, nc, sc, diag = acc[0], acc[1], acc[2], acc[3]
        mid = jnp.full((size, size), inner, jnp.int32) == 1
        table = [
            [zero, ns, nc, zero],
            [ns.T + jnp.where(mid, 0.0, diag), jnp.where(mid, diag, 0.0), sc, zero],
            [nc.T, sc.T, zero, zero],
        ]
        for k in range(4):
            l = jnp.where(side == 0, k, 3 - k)
            for out, flag in zip(outs, (0, 1)):

                @pl.when(((l & 1) ^ gz) == flag)
                def _(k=k, l=l, out=out):
                    for row in range(3):
                        out[(l >> 1) ^ gy, row * size : (row + 1) * size, :] = table[row][k]


def whole(shape):
    return pl.BlockSpec(shape, lambda j, at: (0,) * len(shape))


def call(name, kernel, at, grid, in_specs, operands, out_shapes, scratch=(), types=None):
    types = types or [F32] * len(out_shapes)
    return pl.pallas_call(
        kernel,
        out_shape=tuple(jax.ShapeDtypeStruct(o, t) for o, t in zip(out_shapes, types)),
        grid_spec=pltpu.PrefetchScalarGridSpec(
            num_scalar_prefetch=1,
            grid=(grid,),
            in_specs=in_specs,
            out_specs=tuple(whole(o) for o in out_shapes),
            scratch_shapes=scratch,
        ),
        cost_estimate=pl.CostEstimate(flops=1, transcendentals=0, bytes_accessed=1),
        compiler_params=pltpu.CompilerParams(vmem_limit_bytes=40 << 20),
        name=name,
    )(at, *operands)


def once(name, kernel, at, operands, out_shapes, types=None):
    specs = [whole(o.shape) for o in operands]
    return call(name, kernel, at, 1, specs, operands, out_shapes, types=types)


def add_split_kernel(at, keep, got, first, second):
    first[...] = keep[0] + got[0]
    second[...] = keep[1] + got[1]


def wrapped(cols, lanes):
    return [(lo, min(lo + lanes, cols)) for lo in range(0, cols, lanes)]


def lay(out, start, value):
    few, lanes = value.shape[0], out.shape[1]
    for i, (lo, hi) in enumerate(wrapped(value.shape[1], lanes)):
        row = start + i * few
        out[row : row + few, : hi - lo] = value[:, lo:hi].astype(out.dtype)


def pick(laid, start, few, k):
    row, lane = divmod(k * 128, laid.shape[1])
    row = start + row * few
    return laid[row : row + few, lane : lane + 128].astype(F32)


def home_kernel(at, keep, got, core_keep, core_got, gram_own, to_near, kept, to_cross, to_far):
    rows = gram_own.shape[0]
    to_near[:rows] = (keep[:rows] + got[:rows]).astype(to_near.dtype)
    gram_own[...] = keep[rows : 2 * rows] + got[rows : 2 * rows]
    to_cross[:rows] = (keep[2 * rows :] + got[2 * rows :]).astype(to_cross.dtype)
    lay(to_near, rows, core_keep[0] + core_got[0])
    kept[...] = core_keep[1] + core_got[1]
    lay(to_cross, rows, core_keep[2] + core_got[2])
    lay(to_far, 0, core_keep[3] + core_got[3])


def pack_kernel(at, keep, got, core_give, stay, leave):
    rows = stay.shape[0]
    stay[...] = keep[0] + got[0]
    leave[:rows] = (keep[1] + got[1]).astype(leave.dtype)
    size = (leave.shape[0] - rows) // 4
    for k in range(4):
        lay(leave, rows + k * size, core_give[k])


def part_kernel(at, stay, got, core_keep, near0, cross0, far0, to_far, turned, to_near, kept, to_cross):
    rows = turned.shape[0]
    total = stay[...] + got[:rows].astype(F32)
    to_far[:rows] = total.astype(to_far.dtype)
    turned[...] = total.T.astype(turned.dtype)
    laid = near0.shape[0]
    to_near[:laid] = near0[...]
    to_cross[:laid] = cross0[...]
    to_far[rows:laid] = far0[...]
    few, cols = core_keep.shape[1:]
    size, lanes = kept.shape
    for k, (out, start) in enumerate(((to_near, laid), (kept, 0), (to_cross, laid), (to_far, laid))):
        for i, (lo, hi) in enumerate(wrapped(cols, lanes)):
            row = i * few
            other = got[rows + k * size + row : rows + k * size + row + few, : hi - lo]
            out[start + row : start + row + few, : hi - lo] = (
                core_keep[k, :, lo:hi] + other.astype(F32)
            ).astype(out.dtype)


def final_kernel(inverse, at, own, kept0, far, turned, near, kept1, cross, gram, core):
    rows = own.shape[0]
    side, inner = at[2], at[3]
    gram[...] = (
        (own[...] + near[:rows].astype(F32) + cross[:rows].astype(F32))
        + (far[:rows].astype(F32) + turned[...].astype(F32))
    ) * inverse
    few, nz = core.shape[0], core.shape[2]
    half = core.shape[1] // 2
    early = kept0.shape[1] // 128
    laid = near.shape[0] - kept1.shape[0]
    mid = jnp.full((few, 128), inner, jnp.int32) == 1
    for j in range(half * nz):
        first = j < early
        start, k = (rows, j) if first else (laid, j - early)
        kept = kept0[:, k * 128 : (k + 1) * 128] if first else pick(kept1, 0, few, k)
        mine = jnp.where(mid, kept, pick(near, start, few, k))
        c, z = divmod(j, nz)
        core[:, half * (1 - side) + c, z, :] = mine
        core[:, half * side + c, z, :] = pick(cross, start, few, k) + pick(far, start, few, k)


def pairs(at, near, own, cross, other, carried, last, ny):
    rows, width = near.shape
    first = carried is None
    acc_shape = (4, rows, rows)
    return call(
        "pairs",
        functools.partial(pairs_kernel, first, last),
        at,
        width // ny,
        [pl.BlockSpec((rows, ny), lambda j, at: (0, j))] * 4 + ([] if first else [whole(acc_shape)]),
        [near, own, cross, other] + ([] if first else [carried]),
        [(2, 3 * rows, rows)] * 2 if last else [acc_shape],
        [pltpu.VMEM(acc_shape, F32)],
    )


def meet_kernel(first, last, joined, at, far, near, own, cross, basis, y_own, *rest):
    if not first:
        carried, *rest = rest
    if joined:
        old_keep, old_give, *rest = rest
    *outs, core_keep, core_give, acc = rest
    step = pl.program_id(0)
    gy, gz, side = at[0], at[1], at[2]
    base = 0
    if joined:
        base = old_keep.shape[2]

    @pl.when(step == 0)
    def _():
        acc[...] = jnp.zeros_like(acc) if first else carried[...]
        if joined:
            core_keep[:, :, :base] = old_keep[...]
            core_give[:, :, :base] = old_give[...]

    f, n, s, c = far[...], near[...], own[...], cross[...]
    projected = nn(basis[0], n) + nn(basis[1], s) + nn(basis[2], c) + nn(basis[3], f)
    part = nn(projected.astype(BF16), y_own[...])
    acc[0] += nt(f, n)
    acc[1] += nt(f, s)
    acc[2] += nt(f, c)
    few, cols = part.shape[0] // 8, part.shape[1]
    span = pl.ds(pl.multiple_of(base + step * cols, 128), cols)
    for z in range(4):
        k = jnp.where(side == 0, z, 3 - z)
        for out, flag in ((core_keep, gy), (core_give, 1 - gy)):
            for y in range(2):

                @pl.when(flag == y)
                def _(z=z, k=k, y=y, out=out):
                    start = (2 * z + y) * few
                    out[k, :, span] = part[start : start + few]

    @pl.when(step == pl.num_programs(0) - 1)
    def _():
        if not last:
            outs[0][...] = acc[...]
            return
        for k in range(4):
            l = jnp.where(side == 0, k, 3 - k)
            for out, flag in zip(outs, (0, 1)):

                @pl.when(((l & 1) ^ gz) == flag)
                def _(k=k, l=l, out=out):
                    out[(l >> 1) ^ gy] = acc[k] if k < 3 else jnp.zeros_like(acc[0])


def meet(at, far, skip, n, near, own, cross, lo, basis, y_own, carried, old, last):
    rows = far.shape[0]
    ny, s_cols = y_own.shape
    rank = basis.shape[1]
    first, joined = carried is None, old is not None
    shifted = pl.BlockSpec((rows, ny), lambda j, at: (0, lo + j))
    acc_shape = (3, rows, rows)
    core_shape = (4, rank // 8, n * s_cols + (old[0].shape[2] if joined else 0))
    return call(
        "meet",
        functools.partial(meet_kernel, first, last, joined),
        at,
        n,
        [pl.BlockSpec((rows, ny), lambda j, at: (0, skip + j)), shifted, shifted, shifted]
        + [whole(basis.shape), whole(y_own.shape)]
        + ([] if first else [whole(acc_shape)])
        + ([whole(o.shape) for o in old] if joined else []),
        [far, near, own, cross, basis, y_own]
        + ([] if first else [carried])
        + (list(old) if joined else []),
        ([(2, rows, rows)] * 2 if last else [acc_shape]) + [core_shape] * 2,
        [pltpu.VMEM(acc_shape, F32)],
    )


def meeting(snapshot, x_basis, y_basis):
    rows, ncomp, nz, ny = snapshot.shape
    rank = x_basis.shape[1]
    gx, gy, gz = lax.axis_index("gx"), lax.axis_index("gy"), lax.axis_index("gz")
    side = gx // 2
    inner = (gx == 1) | (gx == 2)
    half = ncomp // 2
    width = nz * ny
    inverse = 1.0 / (ncomp * width * lax.axis_size("gy") * lax.axis_size("gz"))
    own_at, oth_at = (1 - side) * half, side * half
    at = jnp.stack([gy, gz, side, inner.astype(jnp.int32)])

    tied = lax.optimization_barrier

    def take(source, start):
        return lax.dynamic_slice_in_dim(source, start, 1, 1).reshape(rows, nz, ny)

    def flat(a):
        return a.reshape(rows, width)

    near, cross, own, oth = ([None] * half for _ in range(4))
    oth_raw = take(snapshot, oth_at)
    source, oth_raw = tied((snapshot, oth_raw))
    own_raw = take(source, own_at)
    source, own_raw = tied((source, own_raw))
    oth_late = take(source, oth_at + 1)
    source, oth_late = tied((source, oth_late))
    oth[1], own[1] = flat(oth_late), flat(take(source, own_at + 1))
    cross_raw = lax.ppermute(oth_raw, "gx", CROSS)
    near_raw = lax.ppermute(own_raw, "gx", NEAR)
    cross[1] = lax.ppermute(oth[1], "gx", CROSS)
    near[1] = lax.ppermute(own[1], "gx", NEAR)
    oth_raw, own_raw, oth[1], own[1] = tied((oth_raw, own_raw, oth[1], own[1]))
    oth[0], own[0] = flat(oth_raw), flat(own_raw)

    places = [
        jnp.where(side == 0, 0, 3),
        gx,
        jnp.where(side == 0, 2, 1),
        jnp.where(side == 0, 3, 0),
    ]
    basis = jnp.stack([lax.dynamic_slice_in_dim(x_basis, p * rows, rows, 0).T for p in places])
    y_own = lax.dynamic_slice_in_dim(y_basis, gy * ny, ny, 0)

    cuts = [(0, 9), (9, 14), (14, 16)]

    def piece(lo, hi):
        parts = []
        for h in range(half):
            a, b = max(lo, h * nz), min(hi, (h + 1) * nz)
            if a < b:
                parts.append(oth[h] if b - a == nz else oth[h][:, (a - h * nz) * ny : (b - h * nz) * ny])
        return parts[0] if len(parts) == 1 else jnp.concatenate(parts, 1)

    def send_far(i, *gate):
        data, gate = tied((sends[i], gate))
        return lax.ppermute(data, "gx", FAR), *gate

    def meets(i, far, carried, old, last=False):
        lo, hi = cuts[i]
        for h in range(half):
            a, b = max(lo, h * nz), min(hi, (h + 1) * nz)
            if a < b:
                carried, *old = meet(
                    at, far, a - lo, b - a, near[h], own[h], cross[h], a - h * nz,
                    basis, y_own, carried, old, False
                ) if not last else wrap_last(meet(
                    at, far, a - lo, b - a, near[h], own[h], cross[h], a - h * nz,
                    basis, y_own, carried, old, True
                ))
        return carried, *old

    def wrap_last(outs):
        return (outs[0], outs[1]), *outs[2:]

    sends = [piece(lo, hi) for lo, hi in cuts]
    sends, cross_raw, own[0] = tied((sends, cross_raw, own[0]))
    cross[0] = flat(cross_raw)
    cross[0], near_raw = tied((cross[0], near_raw))
    near[0] = flat(near_raw)
    far0, cross[0], near[0], own[0], basis, y_own = send_far(
        0, cross[0], near[0], own[0], basis, y_own
    )
    (sums,) = pairs(at, near[0], own[0], cross[0], oth[0], None, False, ny)
    sums, cross[1] = tied((sums, cross[1]))

    far1, cross[1], near[1], sums = send_far(1, cross[1], near[1], sums)
    keep, give = pairs(at, near[1], own[1], cross[1], oth[1], sums, True, ny)

    early, leave = once(
        "add_split", add_split_kernel, at, [keep, lax.ppermute(give, "gz", SWAP)], [keep.shape[1:]] * 2
    )
    got = lax.ppermute(leave, "gy", SWAP)
    far2, far0 = send_far(2, far0)
    far0, got = tied((far0, got))
    acc, *core = meets(0, far0, None, None)
    core_got = lax.ppermute(core[1], "gy", SWAP)
    few, cols = core_got.shape[1:]
    laid = rows + few * len(wrapped(cols, rows))
    home = once(
        "home",
        home_kernel,
        at,
        [early, got, core[0], core_got],
        [(rows, rows), (laid, rows), (few, cols), (laid, rows), (laid - rows, rows)],
        [F32, BF16, F32, BF16, BF16],
    )
    far1, acc, home = tied((far1, acc, home))
    acc, *core = meets(1, far1, acc, None)
    far2, acc, home = tied((far2, acc, home))
    gram_own, near_home, kept_home, cross_home, far_home = home
    (keep, give), *core = meets(2, far2, acc, core, True)

    few, cols = core[0].shape[1:]
    size = few * len(wrapped(cols, rows))
    stay, leave = once(
        "pack",
        pack_kernel,
        at,
        [keep, lax.ppermute(give, "gz", SWAP), core[1]],
        [(rows, rows), (rows + 4 * size, rows)],
        [F32, BF16],
    )
    full = laid + size
    to_far, turned, to_near, kept, to_cross = once(
        "part",
        part_kernel,
        at,
        [stay, lax.ppermute(leave, "gy", SWAP), core[0], near_home, cross_home, far_home],
        [(full, rows), (rows, rows), (full, rows), (size, rows), (full, rows)],
        [BF16, BF16, BF16, F32, BF16],
    )
    return once(
        "final",
        functools.partial(final_kernel, inverse),
        at,
        [
            gram_own,
            kept_home,
            lax.ppermute(to_far, "gx", FAR_BACK),
            lax.ppermute(turned, ("gx", "gy", "gz"), TURN),
            lax.ppermute(to_near, "gx", NEAR_BACK),
            kept,
            lax.ppermute(to_cross, "gx", CROSS),
        ],
        [(rows, rows), (few, ncomp, nz, y_basis.shape[1])],
    )


def solution(mesh):
    in_specs = (P(("grp", "gx"), None, "gz", "gy"), P("grp", None), P("grp", None))
    out_specs = (P(("grp", "gx"), ("gy", "gz")), P(("grp", "gx", "gy"), None, "gz", None))
    sizes = (mesh.shape["gx"], mesh.shape["gy"], mesh.shape["gz"])
    body = meeting if sizes == (4, 2, 2) else gathered
    return jax.shard_map(body, mesh=mesh, in_specs=in_specs, out_specs=out_specs, check_vma=False)
```

```python
import functools

import jax
import jax.numpy as jnp
from jax import lax
from jax.experimental import pallas as pl
from jax.experimental.pallas import tpu as pltpu
from jax.sharding import PartitionSpec as P

F32 = jnp.float32
BF16 = jnp.bfloat16
NEAR = [(0, 1), (3, 2)]
CROSS = [(1, 2), (2, 1)]
FAR = [(0, 2), (3, 1)]
NEAR_BACK = [(1, 0), (2, 3)]
FAR_BACK = [(1, 3), (2, 0)]
SWAP = [(0, 1), (1, 0)]
TURN = [(4 + l, 4 * l + 3) for l in (0, 1, 2)] + [(8 + l, 4 * l) for l in (1, 2, 3)]


def nt(a, b):
    return lax.dot_general(a, b, (((1,), (1,)), ((), ())), preferred_element_type=F32)


def tn(a, b):
    return lax.dot_general(a, b, (((0,), (0,)), ((), ())), preferred_element_type=F32)


def nn(a, b):
    return jnp.dot(a, b, preferred_element_type=F32)


def gathered(snapshot, x_basis, y_basis):
    rows_local = snapshot.shape[0]
    columns = snapshot.shape[1] * snapshot.shape[2] * snapshot.shape[3]
    unfolded = snapshot.reshape(rows_local, columns)
    rank_count = x_basis.shape[1]
    rank_rows = rank_count // lax.axis_size("gx")
    inverse = 1.0 / (columns * lax.axis_size("gy") * lax.axis_size("gz"))
    basis_cols = lax.dynamic_slice_in_dim(x_basis, lax.axis_index("gx") * rank_rows, rank_rows, 1)
    shard_rows = lax.all_gather(unfolded, "gx", axis=0, tiled=True)
    gram_rows = nt(unfolded, shard_rows)
    own_rows = tn(basis_cols, shard_rows).astype(BF16)
    gram_out = lax.psum_scatter(gram_rows * inverse, ("gy", "gz"), scatter_dimension=1, tiled=True)
    shaped = own_rows.reshape(rank_rows, *snapshot.shape[1:])
    along_y = lax.all_to_all(shaped, "gy", split_axis=0, concat_axis=3, tiled=True)
    core_flat = nn(along_y.reshape(-1, along_y.shape[3]), y_basis)
    return gram_out, core_flat.reshape(*along_y.shape[:3], y_basis.shape[1])


def pairs_kernel(first, last, at, near, own, cross, other, *rest):
    if not first:
        carried, *rest = rest
    *outs, acc = rest
    step = pl.program_id(0)

    @pl.when(step == 0)
    def _():
        acc[...] = jnp.zeros_like(acc) if first else carried[...]

    n, s, c, o = near[...], own[...], cross[...], other[...]
    acc[0] += nt(n, s)
    acc[1] += nt(n, c)
    acc[2] += nt(s, c)
    acc[3] += nt(s, s) + nt(o, o)

    @pl.when(step == pl.num_programs(0) - 1)
    def _():
        if not last:
            outs[0][...] = acc[...]
            return
        gy, gz, side, inner = at[0], at[1], at[2], at[3]
        size = acc.shape[1]
        zero = jnp.zeros((size, size), F32)
        ns, nc, sc, diag = acc[0], acc[1], acc[2], acc[3]
        mid = jnp.full((size, size), inner, jnp.int32) == 1
        table = [
            [zero, ns, nc, zero],
            [ns.T + jnp.where(mid, 0.0, diag), jnp.where(mid, diag, 0.0), sc, zero],
            [nc.T, sc.T, zero, zero],
        ]
        for k in range(4):
            l = jnp.where(side == 0, k, 3 - k)
            for out, flag in zip(outs, (0, 1)):

                @pl.when(((l & 1) ^ gz) == flag)
                def _(k=k, l=l, out=out):
                    for row in range(3):
                        out[(l >> 1) ^ gy, row * size : (row + 1) * size, :] = table[row][k]


def whole(shape):
    return pl.BlockSpec(shape, lambda j, at: (0,) * len(shape))


def call(name, kernel, at, grid, in_specs, operands, out_shapes, scratch=(), types=None):
    types = types or [F32] * len(out_shapes)
    return pl.pallas_call(
        kernel,
        out_shape=tuple(jax.ShapeDtypeStruct(o, t) for o, t in zip(out_shapes, types)),
        grid_spec=pltpu.PrefetchScalarGridSpec(
            num_scalar_prefetch=1,
            grid=(grid,),
            in_specs=in_specs,
            out_specs=tuple(whole(o) for o in out_shapes),
            scratch_shapes=scratch,
        ),
        cost_estimate=pl.CostEstimate(flops=1, transcendentals=0, bytes_accessed=1),
        compiler_params=pltpu.CompilerParams(vmem_limit_bytes=40 << 20),
        name=name,
    )(at, *operands)


def once(name, kernel, at, operands, out_shapes, types=None):
    specs = [whole(o.shape) for o in operands]
    return call(name, kernel, at, 1, specs, operands, out_shapes, types=types)


def add_split_kernel(at, keep, got, first, second):
    first[...] = keep[0] + got[0]
    second[...] = keep[1] + got[1]


def wrapped(cols, lanes):
    return [(lo, min(lo + lanes, cols)) for lo in range(0, cols, lanes)]


def lay(out, start, value):
    few, lanes = value.shape[0], out.shape[1]
    for i, (lo, hi) in enumerate(wrapped(value.shape[1], lanes)):
        row = start + i * few
        out[row : row + few, : hi - lo] = value[:, lo:hi].astype(out.dtype)


def pick(laid, start, few, k):
    row, lane = divmod(k * 128, laid.shape[1])
    row = start + row * few
    return laid[row : row + few, lane : lane + 128].astype(F32)


def home_kernel(at, keep, got, core_keep, core_got, gram_own, to_near, kept, to_cross, to_far):
    rows = gram_own.shape[0]
    to_near[:rows] = (keep[:rows] + got[:rows]).astype(to_near.dtype)
    gram_own[...] = keep[rows : 2 * rows] + got[rows : 2 * rows]
    to_cross[:rows] = (keep[2 * rows :] + got[2 * rows :]).astype(to_cross.dtype)
    lay(to_near, rows, core_keep[0] + core_got[0])
    kept[...] = core_keep[1] + core_got[1]
    lay(to_cross, rows, core_keep[2] + core_got[2])
    lay(to_far, 0, core_keep[3] + core_got[3])


def add_late_kernel(at, keep, got, stay, leave):
    stay[...] = keep[0] + got[0]
    leave[...] = (keep[1] + got[1]).astype(leave.dtype)


def join_kernel(at, keep, got, near0, to_near, kept, to_cross):
    laid = near0.shape[0]
    to_near[:laid] = near0[...]
    lay(to_near, laid, keep[0] + got[0])
    kept[...] = keep[1] + got[1]
    lay(to_cross, 0, keep[2] + got[2])


def part_kernel(at, stay, got, core_keep, core_got, far0, to_far, turned):
    rows = turned.shape[0]
    total = stay[...] + got[...].astype(F32)
    to_far[:rows] = total.astype(to_far.dtype)
    turned[...] = total.T.astype(turned.dtype)
    laid = rows + far0.shape[0]
    to_far[rows:laid] = far0[...]
    lay(to_far, laid, core_keep[3] + core_got[3])


def final_kernel(inverse, at, own, kept0, far, turned, near, kept1, cross0, cross1, gram, core):
    rows = own.shape[0]
    side, inner = at[2], at[3]
    gram[...] = (
        (own[...] + near[:rows].astype(F32) + cross0[:rows].astype(F32))
        + (far[:rows].astype(F32) + turned[...].astype(F32))
    ) * inverse
    few, nz = core.shape[0], core.shape[2]
    half = core.shape[1] // 2
    early = kept0.shape[1] // 128
    few_cols = kept1.shape[1]
    size = few * len(wrapped(few_cols, rows))
    laid = near.shape[0] - size
    mid = jnp.full((few, 128), inner, jnp.int32) == 1
    for j in range(half * nz):
        first = j < early
        start, k = (rows, j) if first else (laid, j - early)
        kept = (kept0 if first else kept1)[:, k * 128 : (k + 1) * 128]
        mine = jnp.where(mid, kept, pick(near, start, few, k))
        c, z = divmod(j, nz)
        core[:, half * (1 - side) + c, z, :] = mine
        cross = pick(cross0, rows, few, k) if first else pick(cross1, 0, few, k)
        core[:, half * side + c, z, :] = cross + pick(far, start, few, k)


def pairs(at, near, own, cross, other, carried, last, ny):
    rows, width = near.shape
    first = carried is None
    acc_shape = (4, rows, rows)
    return call(
        "pairs",
        functools.partial(pairs_kernel, first, last),
        at,
        width // ny,
        [pl.BlockSpec((rows, ny), lambda j, at: (0, j))] * 4 + ([] if first else [whole(acc_shape)]),
        [near, own, cross, other] + ([] if first else [carried]),
        [(2, 3 * rows, rows)] * 2 if last else [acc_shape],
        [pltpu.VMEM(acc_shape, F32)],
    )


def meet_kernel(first, last, joined, at, far, near, own, cross, basis, y_own, *rest):
    if not first:
        carried, *rest = rest
    if joined:
        old_keep, old_give, *rest = rest
    *outs, core_keep, core_give, acc = rest
    step = pl.program_id(0)
    gy, gz, side = at[0], at[1], at[2]
    base = 0
    if joined:
        base = old_keep.shape[2]

    @pl.when(step == 0)
    def _():
        acc[...] = jnp.zeros_like(acc) if first else carried[...]
        if joined:
            core_keep[:, :, :base] = old_keep[...]
            core_give[:, :, :base] = old_give[...]

    f, n, s, c = far[...], near[...], own[...], cross[...]
    projected = nn(basis[0], n) + nn(basis[1], s) + nn(basis[2], c) + nn(basis[3], f)
    part = nn(projected.astype(BF16), y_own[...])
    acc[0] += nt(f, n)
    acc[1] += nt(f, s)
    acc[2] += nt(f, c)
    few, cols = part.shape[0] // 8, part.shape[1]
    span = pl.ds(pl.multiple_of(base + step * cols, 128), cols)
    for z in range(4):
        k = jnp.where(side == 0, z, 3 - z)
        for out, flag in ((core_keep, gy), (core_give, 1 - gy)):
            for y in range(2):

                @pl.when(flag == y)
                def _(z=z, k=k, y=y, out=out):
                    start = (2 * z + y) * few
                    out[k, :, span] = part[start : start + few]

    @pl.when(step == pl.num_programs(0) - 1)
    def _():
        if not last:
            outs[0][...] = acc[...]
            return
        for k in range(4):
            l = jnp.where(side == 0, k, 3 - k)
            for out, flag in zip(outs, (0, 1)):

                @pl.when(((l & 1) ^ gz) == flag)
                def _(k=k, l=l, out=out):
                    out[(l >> 1) ^ gy] = acc[k] if k < 3 else jnp.zeros_like(acc[0])


def meet(at, far, skip, n, near, own, cross, lo, basis, y_own, carried, old, last):
    rows = far.shape[0]
    ny, s_cols = y_own.shape
    rank = basis.shape[1]
    first, joined = carried is None, old is not None
    shifted = pl.BlockSpec((rows, ny), lambda j, at: (0, lo + j))
    acc_shape = (3, rows, rows)
    core_shape = (4, rank // 8, n * s_cols + (old[0].shape[2] if joined else 0))
    return call(
        "meet",
        functools.partial(meet_kernel, first, last, joined),
        at,
        n,
        [pl.BlockSpec((rows, ny), lambda j, at: (0, skip + j)), shifted, shifted, shifted]
        + [whole(basis.shape), whole(y_own.shape)]
        + ([] if first else [whole(acc_shape)])
        + ([whole(o.shape) for o in old] if joined else []),
        [far, near, own, cross, basis, y_own]
        + ([] if first else [carried])
        + (list(old) if joined else []),
        ([(2, rows, rows)] * 2 if last else [acc_shape]) + [core_shape] * 2,
        [pltpu.VMEM(acc_shape, F32)],
    )


def meeting(snapshot, x_basis, y_basis):
    rows, ncomp, nz, ny = snapshot.shape
    rank = x_basis.shape[1]
    gx, gy, gz = lax.axis_index("gx"), lax.axis_index("gy"), lax.axis_index("gz")
    side = gx // 2
    inner = (gx == 1) | (gx == 2)
    half = ncomp // 2
    width = nz * ny
    inverse = 1.0 / (ncomp * width * lax.axis_size("gy") * lax.axis_size("gz"))
    own_at, oth_at = (1 - side) * half, side * half
    at = jnp.stack([gy, gz, side, inner.astype(jnp.int32)])

    tied = lax.optimization_barrier

    def take(source, start):
        return lax.dynamic_slice_in_dim(source, start, 1, 1).reshape(rows, nz, ny)

    def flat(a):
        return a.reshape(rows, width)

    near, cross, own, oth = ([None] * half for _ in range(4))
    oth_raw, own_raw = take(snapshot, oth_at), take(snapshot, own_at)
    source, oth_raw, own_raw = tied((snapshot, oth_raw, own_raw))
    oth_late = take(source, oth_at + 1)
    source, oth_late = tied((source, oth_late))
    oth[1], own[1] = flat(oth_late), flat(take(source, own_at + 1))
    cross_raw = lax.ppermute(oth_raw, "gx", CROSS)
    near_raw = lax.ppermute(own_raw, "gx", NEAR)
    cross[1] = lax.ppermute(oth[1], "gx", CROSS)
    near[1] = lax.ppermute(own[1], "gx", NEAR)
    oth_raw, own_raw, oth[1], own[1] = tied((oth_raw, own_raw, oth[1], own[1]))
    oth[0], own[0] = flat(oth_raw), flat(own_raw)

    places = [
        jnp.where(side == 0, 0, 3),
        gx,
        jnp.where(side == 0, 2, 1),
        jnp.where(side == 0, 3, 0),
    ]
    basis = jnp.stack([lax.dynamic_slice_in_dim(x_basis, p * rows, rows, 0).T for p in places])
    y_own = lax.dynamic_slice_in_dim(y_basis, gy * ny, ny, 0)

    cuts = [(0, 9), (9, 14), (14, 16)]

    def piece(lo, hi):
        parts = []
        for h in range(half):
            a, b = max(lo, h * nz), min(hi, (h + 1) * nz)
            if a < b:
                parts.append(oth[h] if b - a == nz else oth[h][:, (a - h * nz) * ny : (b - h * nz) * ny])
        return parts[0] if len(parts) == 1 else jnp.concatenate(parts, 1)

    def send_far(i, *gate):
        data, gate = tied((sends[i], gate))
        return lax.ppermute(data, "gx", FAR), *gate

    def meets(i, far, carried, old, last=False):
        lo, hi = cuts[i]
        for h in range(half):
            a, b = max(lo, h * nz), min(hi, (h + 1) * nz)
            if a < b:
                carried, *old = meet(
                    at, far, a - lo, b - a, near[h], own[h], cross[h], a - h * nz,
                    basis, y_own, carried, old, False
                ) if not last else wrap_last(meet(
                    at, far, a - lo, b - a, near[h], own[h], cross[h], a - h * nz,
                    basis, y_own, carried, old, True
                ))
        return carried, *old

    def wrap_last(outs):
        return (outs[0], outs[1]), *outs[2:]

    sends = [piece(lo, hi) for lo, hi in cuts]
    sends, cross_raw, own[0] = tied((sends, cross_raw, own[0]))
    cross[0] = flat(cross_raw)
    cross[0], near_raw = tied((cross[0], near_raw))
    near[0] = flat(near_raw)
    far0, cross[0], near[0], own[0], basis, y_own = send_far(
        0, cross[0], near[0], own[0], basis, y_own
    )
    (sums,) = pairs(at, near[0], own[0], cross[0], oth[0], None, False, ny)
    sums, cross[1] = tied((sums, cross[1]))

    far1, cross[1], near[1], sums = send_far(1, cross[1], near[1], sums)
    keep, give = pairs(at, near[1], own[1], cross[1], oth[1], sums, True, ny)

    early, leave = once(
        "add_split", add_split_kernel, at, [keep, lax.ppermute(give, "gz", SWAP)], [keep.shape[1:]] * 2
    )
    got = lax.ppermute(leave, "gy", SWAP)
    far2, far0 = send_far(2, far0)
    far0, got = tied((far0, got))
    acc, *core = meets(0, far0, None, None)
    core_got = lax.ppermute(core[1], "gy", SWAP)
    few, cols = core_got.shape[1:]
    laid = rows + few * len(wrapped(cols, rows))
    home = once(
        "home",
        home_kernel,
        at,
        [early, got, core[0], core_got],
        [(rows, rows), (laid, rows), (few, cols), (laid, rows), (laid - rows, rows)],
        [F32, BF16, F32, BF16, BF16],
    )
    far1, acc, home = tied((far1, acc, home))
    acc, *core = meets(1, far1, acc, None)
    far2, acc, home = tied((far2, acc, home))
    gram_own, near_home, kept_home, cross_home, far_home = home
    (keep, give), *core = meets(2, far2, acc, core, True)

    few, cols = core[0].shape[1:]
    size = few * len(wrapped(cols, rows))
    core_got = lax.ppermute(core[1], "gy", SWAP)
    stay, leave = once(
        "add_late",
        add_late_kernel,
        at,
        [keep, lax.ppermute(give, "gz", SWAP)],
        [(rows, rows)] * 2,
        [F32, BF16],
    )
    full = laid + size
    cross_home = lax.ppermute(cross_home, "gx", CROSS)
    to_near, kept, to_cross = once(
        "join",
        join_kernel,
        at,
        [core[0], core_got, near_home],
        [(full, rows), (few, cols), (size, rows)],
        [BF16, F32, BF16],
    )
    got = lax.ppermute(leave, "gy", SWAP)
    near_got = lax.ppermute(to_near, "gx", NEAR_BACK)
    cross_got = lax.ppermute(to_cross, "gx", CROSS)
    got, cross_home = tied((got, cross_home))
    to_far, turned = once(
        "part",
        part_kernel,
        at,
        [stay, got, core[0], core_got, far_home],
        [(full, rows), (rows, rows)],
        [BF16, BF16],
    )
    return once(
        "final",
        functools.partial(final_kernel, inverse),
        at,
        [
            gram_own,
            kept_home,
            lax.ppermute(to_far, "gx", FAR_BACK),
            lax.ppermute(turned, ("gx", "gy", "gz"), TURN),
            near_got,
            kept,
            cross_home,
            cross_got,
        ],
        [(rows, rows), (few, ncomp, nz, y_basis.shape[1])],
    )


def solution(mesh):
    in_specs = (P(("grp", "gx"), None, "gz", "gy"), P("grp", None), P("grp", None))
    out_specs = (P(("grp", "gx"), ("gy", "gz")), P(("grp", "gx", "gy"), None, "gz", None))
    sizes = (mesh.shape["gx"], mesh.shape["gy"], mesh.shape["gz"])
    body = meeting if sizes == (4, 2, 2) else gathered
    return jax.shard_map(body, mesh=mesh, in_specs=in_specs, out_specs=out_specs, check_vma=False)
```

```python
import functools

import jax
import jax.numpy as jnp
from jax import lax
from jax.experimental import pallas as pl
from jax.experimental.pallas import tpu as pltpu
from jax.sharding import PartitionSpec as P

F32 = jnp.float32
BF16 = jnp.bfloat16
NEAR = [(0, 1), (3, 2)]
CROSS = [(1, 2), (2, 1)]
FAR = [(0, 2), (3, 1)]
NEAR_BACK = [(1, 0), (2, 3)]
FAR_BACK = [(1, 3), (2, 0)]
SWAP = [(0, 1), (1, 0)]
TURN = [(4 + l, 4 * l + 3) for l in (0, 1, 2)] + [(8 + l, 4 * l) for l in (1, 2, 3)]


def nt(a, b):
    return lax.dot_general(a, b, (((1,), (1,)), ((), ())), preferred_element_type=F32)


def tn(a, b):
    return lax.dot_general(a, b, (((0,), (0,)), ((), ())), preferred_element_type=F32)


def nn(a, b):
    return jnp.dot(a, b, preferred_element_type=F32)


def gathered(snapshot, x_basis, y_basis):
    rows_local = snapshot.shape[0]
    columns = snapshot.shape[1] * snapshot.shape[2] * snapshot.shape[3]
    unfolded = snapshot.reshape(rows_local, columns)
    rank_count = x_basis.shape[1]
    rank_rows = rank_count // lax.axis_size("gx")
    inverse = 1.0 / (columns * lax.axis_size("gy") * lax.axis_size("gz"))
    basis_cols = lax.dynamic_slice_in_dim(x_basis, lax.axis_index("gx") * rank_rows, rank_rows, 1)
    shard_rows = lax.all_gather(unfolded, "gx", axis=0, tiled=True)
    gram_rows = nt(unfolded, shard_rows)
    own_rows = tn(basis_cols, shard_rows).astype(BF16)
    gram_out = lax.psum_scatter(gram_rows * inverse, ("gy", "gz"), scatter_dimension=1, tiled=True)
    shaped = own_rows.reshape(rank_rows, *snapshot.shape[1:])
    along_y = lax.all_to_all(shaped, "gy", split_axis=0, concat_axis=3, tiled=True)
    core_flat = nn(along_y.reshape(-1, along_y.shape[3]), y_basis)
    return gram_out, core_flat.reshape(*along_y.shape[:3], y_basis.shape[1])


def pairs_kernel(first, last, at, near, own, cross, other, *rest):
    if not first:
        carried, *rest = rest
    *outs, acc = rest
    step = pl.program_id(0)

    @pl.when(step == 0)
    def _():
        acc[...] = jnp.zeros_like(acc) if first else carried[...]

    n, s, c, o = near[...], own[...], cross[...], other[...]
    acc[0] += nt(n, s)
    acc[1] += nt(n, c)
    acc[2] += nt(s, c)
    acc[3] += nt(s, s) + nt(o, o)

    @pl.when(step == pl.num_programs(0) - 1)
    def _():
        if not last:
            outs[0][...] = acc[...]
            return
        gy, gz, side, inner = at[0], at[1], at[2], at[3]
        size = acc.shape[1]
        zero = jnp.zeros((size, size), F32)
        ns, nc, sc, diag = acc[0], acc[1], acc[2], acc[3]
        mid = jnp.full((size, size), inner, jnp.int32) == 1
        table = [
            [zero, ns, nc, zero],
            [ns.T + jnp.where(mid, 0.0, diag), jnp.where(mid, diag, 0.0), sc, zero],
            [nc.T, sc.T, zero, zero],
        ]
        for k in range(4):
            l = jnp.where(side == 0, k, 3 - k)
            for out, flag in zip(outs, (0, 1)):

                @pl.when(((l & 1) ^ gz) == flag)
                def _(k=k, l=l, out=out):
                    for row in range(3):
                        out[(l >> 1) ^ gy, row * size : (row + 1) * size, :] = table[row][k]


def whole(shape):
    return pl.BlockSpec(shape, lambda j, at: (0,) * len(shape))


def call(name, kernel, at, grid, in_specs, operands, out_shapes, scratch=(), types=None):
    types = types or [F32] * len(out_shapes)
    return pl.pallas_call(
        kernel,
        out_shape=tuple(jax.ShapeDtypeStruct(o, t) for o, t in zip(out_shapes, types)),
        grid_spec=pltpu.PrefetchScalarGridSpec(
            num_scalar_prefetch=1,
            grid=(grid,),
            in_specs=in_specs,
            out_specs=tuple(whole(o) for o in out_shapes),
            scratch_shapes=scratch,
        ),
        cost_estimate=pl.CostEstimate(flops=1, transcendentals=0, bytes_accessed=1),
        compiler_params=pltpu.CompilerParams(vmem_limit_bytes=40 << 20),
        name=name,
    )(at, *operands)


def once(name, kernel, at, operands, out_shapes, types=None):
    specs = [whole(o.shape) for o in operands]
    return call(name, kernel, at, 1, specs, operands, out_shapes, types=types)


def add_split_kernel(at, keep, got, first, second):
    first[...] = keep[0] + got[0]
    second[...] = keep[1] + got[1]


def wrapped(cols, lanes):
    return [(lo, min(lo + lanes, cols)) for lo in range(0, cols, lanes)]


def lay(out, start, value):
    few, lanes = value.shape[0], out.shape[1]
    for i, (lo, hi) in enumerate(wrapped(value.shape[1], lanes)):
        row = start + i * few
        out[row : row + few, : hi - lo] = value[:, lo:hi].astype(out.dtype)


def pick(laid, start, few, k):
    row, lane = divmod(k * 128, laid.shape[1])
    row = start + row * few
    return laid[row : row + few, lane : lane + 128].astype(F32)


def home_kernel(at, keep, got, core_keep, core_got, gram_own, to_near, kept, to_cross, to_far):
    rows = gram_own.shape[0]
    to_near[:rows] = (keep[:rows] + got[:rows]).astype(to_near.dtype)
    gram_own[...] = keep[rows : 2 * rows] + got[rows : 2 * rows]
    to_cross[:rows] = (keep[2 * rows :] + got[2 * rows :]).astype(to_cross.dtype)
    lay(to_near, rows, core_keep[0] + core_got[0])
    kept[...] = core_keep[1] + core_got[1]
    lay(to_cross, rows, core_keep[2] + core_got[2])
    lay(to_far, 0, core_keep[3] + core_got[3])


def add_late_kernel(at, keep, got, stay, leave):
    stay[...] = keep[0] + got[0]
    leave[...] = (keep[1] + got[1]).astype(leave.dtype)


def join_kernel(at, keep, got, near0, to_near, kept, to_cross):
    laid = near0.shape[0]
    to_near[:laid] = near0[...]
    lay(to_near, laid, keep[0] + got[0])
    kept[...] = keep[1] + got[1]
    lay(to_cross, 0, keep[2] + got[2])


def part_kernel(at, stay, got, core_keep, core_got, far0, to_far, turned):
    rows = turned.shape[0]
    total = stay[...] + got[...].astype(F32)
    to_far[:rows] = total.astype(to_far.dtype)
    turned[...] = total.T.astype(turned.dtype)
    laid = rows + far0.shape[0]
    to_far[rows:laid] = far0[...]
    lay(to_far, laid, core_keep[3] + core_got[3])


def final_kernel(inverse, at, own, kept0, far, turned, near, kept1, cross0, cross1, gram, core):
    rows = own.shape[0]
    side, inner = at[2], at[3]
    gram[...] = (
        (own[...] + near[:rows].astype(F32) + cross0[:rows].astype(F32))
        + (far[:rows].astype(F32) + turned[...].astype(F32))
    ) * inverse
    few, nz = core.shape[0], core.shape[2]
    half = core.shape[1] // 2
    early = kept0.shape[1] // 128
    few_cols = kept1.shape[1]
    size = few * len(wrapped(few_cols, rows))
    laid = near.shape[0] - size
    mid = jnp.full((few, 128), inner, jnp.int32) == 1
    for j in range(half * nz):
        first = j < early
        start, k = (rows, j) if first else (laid, j - early)
        kept = (kept0 if first else kept1)[:, k * 128 : (k + 1) * 128]
        mine = jnp.where(mid, kept, pick(near, start, few, k))
        c, z = divmod(j, nz)
        core[:, half * (1 - side) + c, z, :] = mine
        cross = pick(cross0, rows, few, k) if first else pick(cross1, 0, few, k)
        core[:, half * side + c, z, :] = cross + pick(far, start, few, k)


def pairs(at, near, own, cross, other, carried, last, ny):
    rows, width = near.shape
    first = carried is None
    acc_shape = (4, rows, rows)
    return call(
        "pairs",
        functools.partial(pairs_kernel, first, last),
        at,
        width // ny,
        [pl.BlockSpec((rows, ny), lambda j, at: (0, j))] * 4 + ([] if first else [whole(acc_shape)]),
        [near, own, cross, other] + ([] if first else [carried]),
        [(2, 3 * rows, rows)] * 2 if last else [acc_shape],
        [pltpu.VMEM(acc_shape, F32)],
    )


def meet_kernel(first, last, joined, at, far, near, own, cross, basis, y_own, *rest):
    if not first:
        carried, *rest = rest
    if joined:
        old_keep, old_give, *rest = rest
    *outs, core_keep, core_give, acc = rest
    step = pl.program_id(0)
    gy, gz, side = at[0], at[1], at[2]
    base = 0
    if joined:
        base = old_keep.shape[2]

    @pl.when(step == 0)
    def _():
        acc[...] = jnp.zeros_like(acc) if first else carried[...]
        if joined:
            core_keep[:, :, :base] = old_keep[...]
            core_give[:, :, :base] = old_give[...]

    f, n, s, c = far[...], near[...], own[...], cross[...]
    projected = nn(basis[0], n) + nn(basis[1], s) + nn(basis[2], c) + nn(basis[3], f)
    part = nn(projected.astype(BF16), y_own[...])
    acc[0] += nt(f, n)
    acc[1] += nt(f, s)
    acc[2] += nt(f, c)
    few, cols = part.shape[0] // 8, part.shape[1]
    span = pl.ds(pl.multiple_of(base + step * cols, 128), cols)
    for z in range(4):
        k = jnp.where(side == 0, z, 3 - z)
        for out, flag in ((core_keep, gy), (core_give, 1 - gy)):
            for y in range(2):

                @pl.when(flag == y)
                def _(z=z, k=k, y=y, out=out):
                    start = (2 * z + y) * few
                    out[k, :, span] = part[start : start + few]

    @pl.when(step == pl.num_programs(0) - 1)
    def _():
        if not last:
            outs[0][...] = acc[...]
            return
        for k in range(4):
            l = jnp.where(side == 0, k, 3 - k)
            for out, flag in zip(outs, (0, 1)):

                @pl.when(((l & 1) ^ gz) == flag)
                def _(k=k, l=l, out=out):
                    out[(l >> 1) ^ gy] = acc[k] if k < 3 else jnp.zeros_like(acc[0])


def meet(at, far, skip, n, near, own, cross, lo, basis, y_own, carried, old, last):
    rows = far.shape[0]
    ny, s_cols = y_own.shape
    rank = basis.shape[1]
    first, joined = carried is None, old is not None
    shifted = pl.BlockSpec((rows, ny), lambda j, at: (0, lo + j))
    acc_shape = (3, rows, rows)
    core_shape = (4, rank // 8, n * s_cols + (old[0].shape[2] if joined else 0))
    return call(
        "meet",
        functools.partial(meet_kernel, first, last, joined),
        at,
        n,
        [pl.BlockSpec((rows, ny), lambda j, at: (0, skip + j)), shifted, shifted, shifted]
        + [whole(basis.shape), whole(y_own.shape)]
        + ([] if first else [whole(acc_shape)])
        + ([whole(o.shape) for o in old] if joined else []),
        [far, near, own, cross, basis, y_own]
        + ([] if first else [carried])
        + (list(old) if joined else []),
        ([(2, rows, rows)] * 2 if last else [acc_shape]) + [core_shape] * 2,
        [pltpu.VMEM(acc_shape, F32)],
    )


def meeting(snapshot, x_basis, y_basis):
    rows, ncomp, nz, ny = snapshot.shape
    rank = x_basis.shape[1]
    gx, gy, gz = lax.axis_index("gx"), lax.axis_index("gy"), lax.axis_index("gz")
    side = gx // 2
    inner = (gx == 1) | (gx == 2)
    half = ncomp // 2
    width = nz * ny
    inverse = 1.0 / (ncomp * width * lax.axis_size("gy") * lax.axis_size("gz"))
    own_at, oth_at = (1 - side) * half, side * half
    at = jnp.stack([gy, gz, side, inner.astype(jnp.int32)])

    tied = lax.optimization_barrier

    def take(source, start, lo=0, count=rows):
        return lax.dynamic_slice(source, (lo, start, 0, 0), (count, 1, nz, ny)).reshape(count, nz, ny)

    def flat(*parts):
        parts = [a.reshape(a.shape[0], width) for a in parts]
        return parts[0] if len(parts) == 1 else jnp.concatenate(parts, 0)

    near, cross, own, oth = ([None] * half for _ in range(4))
    source = snapshot
    oth_raw, own_raw = [], []
    for lo, count in ((0, rows // 2), (rows // 2, rows - rows // 2)):
        o, w = take(source, oth_at, lo, count), take(source, own_at, lo, count)
        source, o, w = tied((source, o, w))
        oth_raw.append(o)
        own_raw.append(w)
    oth_late = take(source, oth_at + 1)
    source, oth_late = tied((source, oth_late))
    oth[1], own[1] = flat(oth_late), flat(take(source, own_at + 1))
    cross_raw = [lax.ppermute(a, "gx", CROSS) for a in oth_raw]
    near_raw = [lax.ppermute(a, "gx", NEAR) for a in own_raw]
    cross[1] = lax.ppermute(oth[1], "gx", CROSS)
    own[1], cross_raw[0] = tied((own[1], cross_raw[0]))
    near[1] = lax.ppermute(own[1], "gx", NEAR)
    source, oth[1], own[1] = tied((source, oth[1], own[1]))
    oth[0], own[0] = flat(take(source, oth_at)), flat(take(source, own_at))

    places = [
        jnp.where(side == 0, 0, 3),
        gx,
        jnp.where(side == 0, 2, 1),
        jnp.where(side == 0, 3, 0),
    ]
    basis = jnp.stack([lax.dynamic_slice_in_dim(x_basis, p * rows, rows, 0).T for p in places])
    y_own = lax.dynamic_slice_in_dim(y_basis, gy * ny, ny, 0)

    cuts = [(0, 10), (10, 15), (15, 16)]

    def piece(lo, hi):
        parts = []
        for h in range(half):
            a, b = max(lo, h * nz), min(hi, (h + 1) * nz)
            if a < b:
                parts.append(oth[h] if b - a == nz else oth[h][:, (a - h * nz) * ny : (b - h * nz) * ny])
        return parts[0] if len(parts) == 1 else jnp.concatenate(parts, 1)

    def send_far(i, *gate):
        data, gate = tied((sends[i], gate))
        return lax.ppermute(data, "gx", FAR), *gate

    def meets(i, far, carried, old, last=False):
        lo, hi = cuts[i]
        for h in range(half):
            a, b = max(lo, h * nz), min(hi, (h + 1) * nz)
            if a < b:
                carried, *old = meet(
                    at, far, a - lo, b - a, near[h], own[h], cross[h], a - h * nz,
                    basis, y_own, carried, old, False
                ) if not last else wrap_last(meet(
                    at, far, a - lo, b - a, near[h], own[h], cross[h], a - h * nz,
                    basis, y_own, carried, old, True
                ))
        return carried, *old

    def wrap_last(outs):
        return (outs[0], outs[1]), *outs[2:]

    sends = [piece(lo, hi) for lo, hi in cuts]
    sends, cross_raw, own[0] = tied((sends, cross_raw, own[0]))
    top = flat(cross_raw[0])
    top, near_raw[0] = tied((top, near_raw[0]))
    near_top = flat(near_raw[0])
    near_top, cross_raw[1] = tied((near_top, cross_raw[1]))
    cross[0] = jnp.concatenate([top, flat(cross_raw[1])], 0)
    cross[0], near_raw[1] = tied((cross[0], near_raw[1]))
    near[0] = jnp.concatenate([near_top, flat(near_raw[1])], 0)
    far0, cross[0], near[0], own[0], basis, y_own = send_far(
        0, cross[0], near[0], own[0], basis, y_own
    )
    (sums,) = pairs(at, near[0], own[0], cross[0], oth[0], None, False, ny)
    sums, cross[1] = tied((sums, cross[1]))

    far1, cross[1], near[1], sums = send_far(1, cross[1], near[1], sums)
    keep, give = pairs(at, near[1], own[1], cross[1], oth[1], sums, True, ny)

    early, leave = once(
        "add_split", add_split_kernel, at, [keep, lax.ppermute(give, "gz", SWAP)], [keep.shape[1:]] * 2
    )
    got = lax.ppermute(leave, "gy", SWAP)
    far2, far0 = send_far(2, far0)
    far0, got = tied((far0, got))
    acc, *core = meets(0, far0, None, None)
    core_got = lax.ppermute(core[1], "gy", SWAP)
    few, cols = core_got.shape[1:]
    laid = rows + few * len(wrapped(cols, rows))
    home = once(
        "home",
        home_kernel,
        at,
        [early, got, core[0], core_got],
        [(rows, rows), (laid, rows), (few, cols), (laid, rows), (laid - rows, rows)],
        [F32, BF16, F32, BF16, BF16],
    )
    far1, acc, home = tied((far1, acc, home))
    acc, *core = meets(1, far1, acc, None)
    far2, acc, home = tied((far2, acc, home))
    gram_own, near_home, kept_home, cross_home, far_home = home
    (keep, give), *core = meets(2, far2, acc, core, True)

    few, cols = core[0].shape[1:]
    size = few * len(wrapped(cols, rows))
    core_got = lax.ppermute(core[1], "gy", SWAP)
    stay, leave = once(
        "add_late",
        add_late_kernel,
        at,
        [keep, lax.ppermute(give, "gz", SWAP)],
        [(rows, rows)] * 2,
        [F32, BF16],
    )
    full = laid + size
    cross_home = lax.ppermute(cross_home, "gx", CROSS)
    to_near, kept, to_cross = once(
        "join",
        join_kernel,
        at,
        [core[0], core_got, near_home],
        [(full, rows), (few, cols), (size, rows)],
        [BF16, F32, BF16],
    )
    got = lax.ppermute(leave, "gy", SWAP)
    near_got = lax.ppermute(to_near, "gx", NEAR_BACK)
    cross_got = lax.ppermute(to_cross, "gx", CROSS)
    got, cross_home = tied((got, cross_home))
    to_far, turned = once(
        "part",
        part_kernel,
        at,
        [stay, got, core[0], core_got, far_home],
        [(full, rows), (rows, rows)],
        [BF16, BF16],
    )
    return once(
        "final",
        functools.partial(final_kernel, inverse),
        at,
        [
            gram_own,
            kept_home,
            lax.ppermute(to_far, "gx", FAR_BACK),
            lax.ppermute(turned, ("gx", "gy", "gz"), TURN),
            near_got,
            kept,
            cross_home,
            cross_got,
        ],
        [(rows, rows), (few, ncomp, nz, y_basis.shape[1])],
    )


def solution(mesh):
    in_specs = (P(("grp", "gx"), None, "gz", "gy"), P("grp", None), P("grp", None))
    out_specs = (P(("grp", "gx"), ("gy", "gz")), P(("grp", "gx", "gy"), None, "gz", None))
    sizes = (mesh.shape["gx"], mesh.shape["gy"], mesh.shape["gz"])
    body = meeting if sizes == (4, 2, 2) else gathered
    return jax.shard_map(body, mesh=mesh, in_specs=in_specs, out_specs=out_specs, check_vma=False)
```

```python
import functools

import jax
import jax.numpy as jnp
from jax import lax
from jax.experimental import pallas as pl
from jax.experimental.pallas import tpu as pltpu
from jax.sharding import PartitionSpec as P

F32 = jnp.float32
BF16 = jnp.bfloat16
NEAR = [(0, 1), (3, 2)]
CROSS = [(1, 2), (2, 1)]
FAR = [(0, 2), (3, 1)]
NEAR_BACK = [(1, 0), (2, 3)]
FAR_BACK = [(1, 3), (2, 0)]
SWAP = [(0, 1), (1, 0)]
TURN = [(4 + l, 4 * l + 3) for l in (0, 1, 2)] + [(8 + l, 4 * l) for l in (1, 2, 3)]


def nt(a, b):
    return lax.dot_general(a, b, (((1,), (1,)), ((), ())), preferred_element_type=F32)


def tn(a, b):
    return lax.dot_general(a, b, (((0,), (0,)), ((), ())), preferred_element_type=F32)


def nn(a, b):
    return jnp.dot(a, b, preferred_element_type=F32)


def gathered(snapshot, x_basis, y_basis):
    rows_local = snapshot.shape[0]
    columns = snapshot.shape[1] * snapshot.shape[2] * snapshot.shape[3]
    unfolded = snapshot.reshape(rows_local, columns)
    rank_count = x_basis.shape[1]
    rank_rows = rank_count // lax.axis_size("gx")
    inverse = 1.0 / (columns * lax.axis_size("gy") * lax.axis_size("gz"))
    basis_cols = lax.dynamic_slice_in_dim(x_basis, lax.axis_index("gx") * rank_rows, rank_rows, 1)
    shard_rows = lax.all_gather(unfolded, "gx", axis=0, tiled=True)
    gram_rows = nt(unfolded, shard_rows)
    own_rows = tn(basis_cols, shard_rows).astype(BF16)
    gram_out = lax.psum_scatter(gram_rows * inverse, ("gy", "gz"), scatter_dimension=1, tiled=True)
    shaped = own_rows.reshape(rank_rows, *snapshot.shape[1:])
    along_y = lax.all_to_all(shaped, "gy", split_axis=0, concat_axis=3, tiled=True)
    core_flat = nn(along_y.reshape(-1, along_y.shape[3]), y_basis)
    return gram_out, core_flat.reshape(*along_y.shape[:3], y_basis.shape[1])


def pairs_kernel(first, last, at, near, own, cross, other, *rest):
    if not first:
        carried, *rest = rest
    *outs, acc = rest
    step = pl.program_id(0)

    @pl.when(step == 0)
    def _():
        acc[...] = jnp.zeros_like(acc) if first else carried[...]

    n, s, c, o = near[...], own[...], cross[...], other[...]
    acc[0] += nt(n, s)
    acc[1] += nt(n, c)
    acc[2] += nt(s, c)
    acc[3] += nt(s, s) + nt(o, o)

    @pl.when(step == pl.num_programs(0) - 1)
    def _():
        if not last:
            outs[0][...] = acc[...]
            return
        gy, gz, side, inner = at[0], at[1], at[2], at[3]
        size = acc.shape[1]
        zero = jnp.zeros((size, size), F32)
        ns, nc, sc, diag = acc[0], acc[1], acc[2], acc[3]
        mid = jnp.full((size, size), inner, jnp.int32) == 1
        table = [
            [zero, ns, nc, zero],
            [ns.T + jnp.where(mid, 0.0, diag), jnp.where(mid, diag, 0.0), sc, zero],
            [nc.T, sc.T, zero, zero],
        ]
        for k in range(4):
            l = jnp.where(side == 0, k, 3 - k)
            for out, flag in zip(outs, (0, 1)):

                @pl.when(((l & 1) ^ gz) == flag)
                def _(k=k, l=l, out=out):
                    for row in range(3):
                        out[(l >> 1) ^ gy, row * size : (row + 1) * size, :] = table[row][k]


def whole(shape):
    return pl.BlockSpec(shape, lambda j, at: (0,) * len(shape))


def call(name, kernel, at, grid, in_specs, operands, out_shapes, scratch=(), types=None):
    types = types or [F32] * len(out_shapes)
    return pl.pallas_call(
        kernel,
        out_shape=tuple(jax.ShapeDtypeStruct(o, t) for o, t in zip(out_shapes, types)),
        grid_spec=pltpu.PrefetchScalarGridSpec(
            num_scalar_prefetch=1,
            grid=(grid,),
            in_specs=in_specs,
            out_specs=tuple(whole(o) for o in out_shapes),
            scratch_shapes=scratch,
        ),
        cost_estimate=pl.CostEstimate(flops=1, transcendentals=0, bytes_accessed=1),
        compiler_params=pltpu.CompilerParams(vmem_limit_bytes=40 << 20),
        name=name,
    )(at, *operands)


def once(name, kernel, at, operands, out_shapes, types=None):
    specs = [whole(o.shape) for o in operands]
    return call(name, kernel, at, 1, specs, operands, out_shapes, types=types)


def add_split_kernel(at, keep, got, first, second):
    first[...] = keep[0] + got[0]
    second[...] = keep[1] + got[1]


def wrapped(cols, lanes):
    return [(lo, min(lo + lanes, cols)) for lo in range(0, cols, lanes)]


def lay(out, start, value):
    few, lanes = value.shape[0], out.shape[1]
    for i, (lo, hi) in enumerate(wrapped(value.shape[1], lanes)):
        row = start + i * few
        out[row : row + few, : hi - lo] = value[:, lo:hi].astype(out.dtype)


def pick(laid, start, few, k):
    row, lane = divmod(k * 128, laid.shape[1])
    row = start + row * few
    return laid[row : row + few, lane : lane + 128].astype(F32)


def home_kernel(at, keep, got, core_keep, core_got, gram_own, to_near, kept, to_cross, to_far):
    rows = gram_own.shape[0]
    to_near[:rows] = (keep[:rows] + got[:rows]).astype(to_near.dtype)
    gram_own[...] = keep[rows : 2 * rows] + got[rows : 2 * rows]
    to_cross[:rows] = (keep[2 * rows :] + got[2 * rows :]).astype(to_cross.dtype)
    lay(to_near, rows, core_keep[0] + core_got[0])
    kept[...] = core_keep[1] + core_got[1]
    lay(to_cross, rows, core_keep[2] + core_got[2])
    lay(to_far, 0, core_keep[3] + core_got[3])


def add_late_kernel(at, keep, got, stay, leave):
    stay[...] = keep[0] + got[0]
    leave[...] = (keep[1] + got[1]).astype(leave.dtype)


def join_kernel(at, keep, got, near0, to_near, kept, to_cross):
    laid = near0.shape[0]
    to_near[:laid] = near0[...]
    lay(to_near, laid, keep[0] + got[0])
    kept[...] = keep[1] + got[1]
    lay(to_cross, 0, keep[2] + got[2])


def part_kernel(at, stay, got, core_keep, core_got, far0, to_far, turned):
    rows = turned.shape[0]
    total = stay[...] + got[...].astype(F32)
    to_far[:rows] = total.astype(to_far.dtype)
    turned[...] = total.T.astype(turned.dtype)
    laid = rows + far0.shape[0]
    to_far[rows:laid] = far0[...]
    lay(to_far, laid, core_keep[3] + core_got[3])


def final_kernel(inverse, at, own, kept0, far, turned, near, kept1, cross0, cross1, gram, core):
    rows = own.shape[0]
    side, inner = at[2], at[3]
    gram[...] = (
        (own[...] + near[:rows].astype(F32) + cross0[:rows].astype(F32))
        + (far[:rows].astype(F32) + turned[...].astype(F32))
    ) * inverse
    few, nz = core.shape[0], core.shape[2]
    half = core.shape[1] // 2
    early = kept0.shape[1] // 128
    few_cols = kept1.shape[1]
    size = few * len(wrapped(few_cols, rows))
    laid = near.shape[0] - size
    mid = jnp.full((few, 128), inner, jnp.int32) == 1
    for j in range(half * nz):
        first = j < early
        start, k = (rows, j) if first else (laid, j - early)
        kept = (kept0 if first else kept1)[:, k * 128 : (k + 1) * 128]
        mine = jnp.where(mid, kept, pick(near, start, few, k))
        c, z = divmod(j, nz)
        core[:, half * (1 - side) + c, z, :] = mine
        cross = pick(cross0, rows, few, k) if first else pick(cross1, 0, few, k)
        core[:, half * side + c, z, :] = cross + pick(far, start, few, k)


def pairs(at, near, own, cross, other, carried, last, ny):
    rows, width = near.shape
    first = carried is None
    acc_shape = (4, rows, rows)
    return call(
        "pairs",
        functools.partial(pairs_kernel, first, last),
        at,
        width // ny,
        [pl.BlockSpec((rows, ny), lambda j, at: (0, j))] * 4 + ([] if first else [whole(acc_shape)]),
        [near, own, cross, other] + ([] if first else [carried]),
        [(2, 3 * rows, rows)] * 2 if last else [acc_shape],
        [pltpu.VMEM(acc_shape, F32)],
    )


def meet_kernel(first, last, joined, at, far, near, own, cross, basis, y_own, *rest):
    if not first:
        carried, *rest = rest
    if joined:
        old_keep, old_give, *rest = rest
    *outs, core_keep, core_give, acc = rest
    step = pl.program_id(0)
    gy, gz, side = at[0], at[1], at[2]
    base = 0
    if joined:
        base = old_keep.shape[2]

    @pl.when(step == 0)
    def _():
        acc[...] = jnp.zeros_like(acc) if first else carried[...]
        if joined:
            core_keep[:, :, :base] = old_keep[...]
            core_give[:, :, :base] = old_give[...]

    f, n, s, c = far[...], near[...], own[...], cross[...]
    projected = nn(basis[0], n) + nn(basis[1], s) + nn(basis[2], c) + nn(basis[3], f)
    part = nn(projected.astype(BF16), y_own[...])
    acc[0] += nt(f, n)
    acc[1] += nt(f, s)
    acc[2] += nt(f, c)
    few, cols = part.shape[0] // 8, part.shape[1]
    span = pl.ds(pl.multiple_of(base + step * cols, 128), cols)
    for z in range(4):
        k = jnp.where(side == 0, z, 3 - z)
        for out, flag in ((core_keep, gy), (core_give, 1 - gy)):
            for y in range(2):

                @pl.when(flag == y)
                def _(z=z, k=k, y=y, out=out):
                    start = (2 * z + y) * few
                    out[k, :, span] = part[start : start + few]

    @pl.when(step == pl.num_programs(0) - 1)
    def _():
        if not last:
            outs[0][...] = acc[...]
            return
        for k in range(4):
            l = jnp.where(side == 0, k, 3 - k)
            for out, flag in zip(outs, (0, 1)):

                @pl.when(((l & 1) ^ gz) == flag)
                def _(k=k, l=l, out=out):
                    out[(l >> 1) ^ gy] = acc[k] if k < 3 else jnp.zeros_like(acc[0])


def meet(at, far, skip, n, near, own, cross, lo, basis, y_own, carried, old, last):
    rows = far.shape[0]
    ny, s_cols = y_own.shape
    rank = basis.shape[1]
    first, joined = carried is None, old is not None
    shifted = pl.BlockSpec((rows, ny), lambda j, at: (0, lo + j))
    acc_shape = (3, rows, rows)
    core_shape = (4, rank // 8, n * s_cols + (old[0].shape[2] if joined else 0))
    return call(
        "meet",
        functools.partial(meet_kernel, first, last, joined),
        at,
        n,
        [pl.BlockSpec((rows, ny), lambda j, at: (0, skip + j)), shifted, shifted, shifted]
        + [whole(basis.shape), whole(y_own.shape)]
        + ([] if first else [whole(acc_shape)])
        + ([whole(o.shape) for o in old] if joined else []),
        [far, near, own, cross, basis, y_own]
        + ([] if first else [carried])
        + (list(old) if joined else []),
        ([(2, rows, rows)] * 2 if last else [acc_shape]) + [core_shape] * 2,
        [pltpu.VMEM(acc_shape, F32)],
    )


def meeting(snapshot, x_basis, y_basis):
    rows, ncomp, nz, ny = snapshot.shape
    rank = x_basis.shape[1]
    gx, gy, gz = lax.axis_index("gx"), lax.axis_index("gy"), lax.axis_index("gz")
    side = gx // 2
    inner = (gx == 1) | (gx == 2)
    half = ncomp // 2
    width = nz * ny
    inverse = 1.0 / (ncomp * width * lax.axis_size("gy") * lax.axis_size("gz"))
    own_at, oth_at = (1 - side) * half, side * half
    at = jnp.stack([gy, gz, side, inner.astype(jnp.int32)])

    tied = lax.optimization_barrier

    def take(source, start, lo=0, count=rows):
        return lax.dynamic_slice(source, (lo, start, 0, 0), (count, 1, nz, ny)).reshape(count, nz, ny)

    def flat(*parts):
        parts = [a.reshape(a.shape[0], width) for a in parts]
        return parts[0] if len(parts) == 1 else jnp.concatenate(parts, 0)

    near, cross, own, oth = ([None] * half for _ in range(4))
    source = snapshot
    oth_raw, own_raw = [], []
    for lo, count in ((0, rows // 2), (rows // 2, rows - rows // 2)):
        o, w = take(source, oth_at, lo, count), take(source, own_at, lo, count)
        source, o, w = tied((source, o, w))
        oth_raw.append(o)
        own_raw.append(w)
    oth_late = take(source, oth_at + 1)
    source, oth_late = tied((source, oth_late))
    oth[1], own[1] = flat(oth_late), flat(take(source, own_at + 1))
    cross_raw = [lax.ppermute(a, "gx", CROSS) for a in oth_raw]
    near_raw = [lax.ppermute(a, "gx", NEAR) for a in own_raw]
    cross[1] = lax.ppermute(oth[1], "gx", CROSS)
    own[1], cross_raw[0] = tied((own[1], cross_raw[0]))
    near[1] = lax.ppermute(own[1], "gx", NEAR)
    source, oth[1], own[1] = tied((source, oth[1], own[1]))
    oth[0], own[0] = flat(take(source, oth_at)), flat(take(source, own_at))

    places = [
        jnp.where(side == 0, 0, 3),
        gx,
        jnp.where(side == 0, 2, 1),
        jnp.where(side == 0, 3, 0),
    ]
    basis = jnp.stack([lax.dynamic_slice_in_dim(x_basis, p * rows, rows, 0).T for p in places])
    y_own = lax.dynamic_slice_in_dim(y_basis, gy * ny, ny, 0)

    cuts = [(0, 10), (10, 14), (14, 16)]

    def piece(lo, hi):
        parts = []
        for h in range(half):
            a, b = max(lo, h * nz), min(hi, (h + 1) * nz)
            if a < b:
                parts.append(oth[h] if b - a == nz else oth[h][:, (a - h * nz) * ny : (b - h * nz) * ny])
        return parts[0] if len(parts) == 1 else jnp.concatenate(parts, 1)

    def send_far(i, *gate):
        data, gate = tied((sends[i], gate))
        return lax.ppermute(data, "gx", FAR), *gate

    def meets(i, far, carried, old, last=False):
        lo, hi = cuts[i]
        for h in range(half):
            a, b = max(lo, h * nz), min(hi, (h + 1) * nz)
            if a < b:
                carried, *old = meet(
                    at, far, a - lo, b - a, near[h], own[h], cross[h], a - h * nz,
                    basis, y_own, carried, old, False
                ) if not last else wrap_last(meet(
                    at, far, a - lo, b - a, near[h], own[h], cross[h], a - h * nz,
                    basis, y_own, carried, old, True
                ))
        return carried, *old

    def wrap_last(outs):
        return (outs[0], outs[1]), *outs[2:]

    sends = [piece(lo, hi) for lo, hi in cuts]
    sends, cross_raw, own[0] = tied((sends, cross_raw, own[0]))
    top = flat(cross_raw[0])
    top, near_raw[0] = tied((top, near_raw[0]))
    near_top = flat(near_raw[0])
    near_top, cross_raw[1] = tied((near_top, cross_raw[1]))
    cross[0] = jnp.concatenate([top, flat(cross_raw[1])], 0)
    cross[0], near_raw[1] = tied((cross[0], near_raw[1]))
    near[0] = jnp.concatenate([near_top, flat(near_raw[1])], 0)
    far0, cross[0], near[0], own[0], basis, y_own = send_far(
        0, cross[0], near[0], own[0], basis, y_own
    )
    (sums,) = pairs(at, near[0], own[0], cross[0], oth[0], None, False, ny)
    sums, cross[1] = tied((sums, cross[1]))

    far1, cross[1], near[1], sums = send_far(1, cross[1], near[1], sums)
    keep, give = pairs(at, near[1], own[1], cross[1], oth[1], sums, True, ny)

    early, leave = once(
        "add_split", add_split_kernel, at, [keep, lax.ppermute(give, "gz", SWAP)], [keep.shape[1:]] * 2
    )
    got = lax.ppermute(leave, "gy", SWAP)
    far2, far0 = send_far(2, far0)
    far0, got = tied((far0, got))
    acc, *core = meets(0, far0, None, None)
    core_got = lax.ppermute(core[1], "gy", SWAP)
    few, cols = core_got.shape[1:]
    laid = rows + few * len(wrapped(cols, rows))
    home = once(
        "home",
        home_kernel,
        at,
        [early, got, core[0], core_got],
        [(rows, rows), (laid, rows), (few, cols), (laid, rows), (laid - rows, rows)],
        [F32, BF16, F32, BF16, BF16],
    )
    far1, acc, home = tied((far1, acc, home))
    acc, *core = meets(1, far1, acc, None)
    far2, acc, home = tied((far2, acc, home))
    gram_own, near_home, kept_home, cross_home, far_home = home
    (keep, give), *core = meets(2, far2, acc, core, True)

    few, cols = core[0].shape[1:]
    size = few * len(wrapped(cols, rows))
    core_got = lax.ppermute(core[1], "gy", SWAP)
    stay, leave = once(
        "add_late",
        add_late_kernel,
        at,
        [keep, lax.ppermute(give, "gz", SWAP)],
        [(rows, rows)] * 2,
        [F32, BF16],
    )
    full = laid + size
    cross_home = lax.ppermute(cross_home, "gx", CROSS)
    to_near, kept, to_cross = once(
        "join",
        join_kernel,
        at,
        [core[0], core_got, near_home],
        [(full, rows), (few, cols), (size, rows)],
        [BF16, F32, BF16],
    )
    got = lax.ppermute(leave, "gy", SWAP)
    near_got = lax.ppermute(to_near, "gx", NEAR_BACK)
    cross_got = lax.ppermute(to_cross, "gx", CROSS)
    got, cross_home = tied((got, cross_home))
    to_far, turned = once(
        "part",
        part_kernel,
        at,
        [stay, got, core[0], core_got, far_home],
        [(full, rows), (rows, rows)],
        [BF16, BF16],
    )
    return once(
        "final",
        functools.partial(final_kernel, inverse),
        at,
        [
            gram_own,
            kept_home,
            lax.ppermute(to_far, "gx", FAR_BACK),
            lax.ppermute(turned, ("gx", "gy", "gz"), TURN),
            near_got,
            kept,
            cross_home,
            cross_got,
        ],
        [(rows, rows), (few, ncomp, nz, y_basis.shape[1])],
    )


def solution(mesh):
    in_specs = (P(("grp", "gx"), None, "gz", "gy"), P("grp", None), P("grp", None))
    out_specs = (P(("grp", "gx"), ("gy", "gz")), P(("grp", "gx", "gy"), None, "gz", None))
    sizes = (mesh.shape["gx"], mesh.shape["gy"], mesh.shape["gz"])
    body = meeting if sizes == (4, 2, 2) else gathered
    return jax.shard_map(body, mesh=mesh, in_specs=in_specs, out_specs=out_specs, check_vma=False)
```

```python
import functools

import jax
import jax.numpy as jnp
from jax import lax
from jax.experimental import pallas as pl
from jax.experimental.pallas import tpu as pltpu
from jax.sharding import PartitionSpec as P

F32 = jnp.float32
BF16 = jnp.bfloat16
NEAR = [(0, 1), (3, 2)]
CROSS = [(1, 2), (2, 1)]
FAR = [(0, 2), (3, 1)]
NEAR_BACK = [(1, 0), (2, 3)]
FAR_BACK = [(1, 3), (2, 0)]
SWAP = [(0, 1), (1, 0)]
TURN = [(4 + l, 4 * l + 3) for l in (0, 1, 2)] + [(8 + l, 4 * l) for l in (1, 2, 3)]


def nt(a, b):
    return lax.dot_general(a, b, (((1,), (1,)), ((), ())), preferred_element_type=F32)


def tn(a, b):
    return lax.dot_general(a, b, (((0,), (0,)), ((), ())), preferred_element_type=F32)


def nn(a, b):
    return jnp.dot(a, b, preferred_element_type=F32)


def gathered(snapshot, x_basis, y_basis):
    rows_local = snapshot.shape[0]
    columns = snapshot.shape[1] * snapshot.shape[2] * snapshot.shape[3]
    unfolded = snapshot.reshape(rows_local, columns)
    rank_count = x_basis.shape[1]
    rank_rows = rank_count // lax.axis_size("gx")
    inverse = 1.0 / (columns * lax.axis_size("gy") * lax.axis_size("gz"))
    basis_cols = lax.dynamic_slice_in_dim(x_basis, lax.axis_index("gx") * rank_rows, rank_rows, 1)
    shard_rows = lax.all_gather(unfolded, "gx", axis=0, tiled=True)
    gram_rows = nt(unfolded, shard_rows)
    own_rows = tn(basis_cols, shard_rows).astype(BF16)
    gram_out = lax.psum_scatter(gram_rows * inverse, ("gy", "gz"), scatter_dimension=1, tiled=True)
    shaped = own_rows.reshape(rank_rows, *snapshot.shape[1:])
    along_y = lax.all_to_all(shaped, "gy", split_axis=0, concat_axis=3, tiled=True)
    core_flat = nn(along_y.reshape(-1, along_y.shape[3]), y_basis)
    return gram_out, core_flat.reshape(*along_y.shape[:3], y_basis.shape[1])


def pairs_kernel(first, last, at, near, own, cross, other, *rest):
    if not first:
        carried, *rest = rest
    *outs, acc = rest
    step = pl.program_id(0)

    @pl.when(step == 0)
    def _():
        acc[...] = jnp.zeros_like(acc) if first else carried[...]

    n, s, c, o = near[...], own[...], cross[...], other[...]
    acc[0] += nt(n, s)
    acc[1] += nt(n, c)
    acc[2] += nt(s, c)
    acc[3] += nt(s, s) + nt(o, o)

    @pl.when(step == pl.num_programs(0) - 1)
    def _():
        if not last:
            outs[0][...] = acc[...]
            return
        gy, gz, side, inner = at[0], at[1], at[2], at[3]
        size = acc.shape[1]
        zero = jnp.zeros((size, size), F32)
        ns, nc, sc, diag = acc[0], acc[1], acc[2], acc[3]
        mid = jnp.full((size, size), inner, jnp.int32) == 1
        table = [
            [zero, ns, nc, zero],
            [ns.T + jnp.where(mid, 0.0, diag), jnp.where(mid, diag, 0.0), sc, zero],
            [nc.T, sc.T, zero, zero],
        ]
        for k in range(4):
            l = jnp.where(side == 0, k, 3 - k)
            for out, flag in zip(outs, (0, 1)):

                @pl.when(((l & 1) ^ gz) == flag)
                def _(k=k, l=l, out=out):
                    for row in range(3):
                        out[(l >> 1) ^ gy, row * size : (row + 1) * size, :] = table[row][k]


def whole(shape):
    return pl.BlockSpec(shape, lambda j, at: (0,) * len(shape))


def call(name, kernel, at, grid, in_specs, operands, out_shapes, scratch=(), types=None):
    types = types or [F32] * len(out_shapes)
    return pl.pallas_call(
        kernel,
        out_shape=tuple(jax.ShapeDtypeStruct(o, t) for o, t in zip(out_shapes, types)),
        grid_spec=pltpu.PrefetchScalarGridSpec(
            num_scalar_prefetch=1,
            grid=(grid,),
            in_specs=in_specs,
            out_specs=tuple(whole(o) for o in out_shapes),
            scratch_shapes=scratch,
        ),
        cost_estimate=pl.CostEstimate(flops=1, transcendentals=0, bytes_accessed=1),
        compiler_params=pltpu.CompilerParams(vmem_limit_bytes=16 << 20),
        name=name,
    )(at, *operands)


def once(name, kernel, at, operands, out_shapes, types=None):
    specs = [whole(o.shape) for o in operands]
    return call(name, kernel, at, 1, specs, operands, out_shapes, types=types)


def add_split_kernel(at, keep, got, first, second):
    first[...] = keep[0] + got[0]
    second[...] = keep[1] + got[1]


def wrapped(cols, lanes):
    return [(lo, min(lo + lanes, cols)) for lo in range(0, cols, lanes)]


def lay(out, start, value):
    few, lanes = value.shape[0], out.shape[1]
    for i, (lo, hi) in enumerate(wrapped(value.shape[1], lanes)):
        row = start + i * few
        out[row : row + few, : hi - lo] = value[:, lo:hi].astype(out.dtype)


def pick(laid, start, few, k):
    row, lane = divmod(k * 128, laid.shape[1])
    row = start + row * few
    return laid[row : row + few, lane : lane + 128].astype(F32)


def home_kernel(at, keep, got, core_keep, core_got, gram_own, to_near, kept, to_cross, to_far):
    rows = gram_own.shape[0]
    to_near[:rows] = (keep[:rows] + got[:rows]).astype(to_near.dtype)
    gram_own[...] = keep[rows : 2 * rows] + got[rows : 2 * rows]
    to_cross[:rows] = (keep[2 * rows :] + got[2 * rows :]).astype(to_cross.dtype)
    lay(to_near, rows, core_keep[0] + core_got[0])
    kept[...] = core_keep[1] + core_got[1]
    lay(to_cross, rows, core_keep[2] + core_got[2])
    lay(to_far, 0, core_keep[3] + core_got[3])


def add_late_kernel(at, keep, got, stay, leave):
    stay[...] = keep[0] + got[0]
    leave[...] = (keep[1] + got[1]).astype(leave.dtype)


def join_kernel(at, keep, got, near0, to_near, kept, to_cross):
    laid = near0.shape[0]
    to_near[:laid] = near0[...]
    lay(to_near, laid, keep[0] + got[0])
    kept[...] = keep[1] + got[1]
    lay(to_cross, 0, keep[2] + got[2])


def part_kernel(at, stay, got, core_keep, core_got, far0, to_far, turned):
    rows = turned.shape[0]
    total = stay[...] + got[...].astype(F32)
    to_far[:rows] = total.astype(to_far.dtype)
    turned[...] = total.T.astype(turned.dtype)
    laid = rows + far0.shape[0]
    to_far[rows:laid] = far0[...]
    lay(to_far, laid, core_keep[3] + core_got[3])


def final_kernel(inverse, at, own, kept0, far, turned, near, kept1, cross0, cross1, gram, core):
    rows = own.shape[0]
    side, inner = at[2], at[3]
    gram[...] = (
        (own[...] + near[:rows].astype(F32) + cross0[:rows].astype(F32))
        + (far[:rows].astype(F32) + turned[...].astype(F32))
    ) * inverse
    few, nz = core.shape[0], core.shape[2]
    half = core.shape[1] // 2
    early = kept0.shape[1] // 128
    few_cols = kept1.shape[1]
    size = few * len(wrapped(few_cols, rows))
    laid = near.shape[0] - size
    mid = jnp.full((few, 128), inner, jnp.int32) == 1
    for j in range(half * nz):
        first = j < early
        start, k = (rows, j) if first else (laid, j - early)
        kept = (kept0 if first else kept1)[:, k * 128 : (k + 1) * 128]
        mine = jnp.where(mid, kept, pick(near, start, few, k))
        c, z = divmod(j, nz)
        core[:, half * (1 - side) + c, z, :] = mine
        cross = pick(cross0, rows, few, k) if first else pick(cross1, 0, few, k)
        core[:, half * side + c, z, :] = cross + pick(far, start, few, k)


def pairs(at, near, own, cross, other, carried, last, ny):
    rows, width = near.shape
    first = carried is None
    acc_shape = (4, rows, rows)
    return call(
        "pairs",
        functools.partial(pairs_kernel, first, last),
        at,
        width // ny,
        [pl.BlockSpec((rows, ny), lambda j, at: (0, j))] * 4 + ([] if first else [whole(acc_shape)]),
        [near, own, cross, other] + ([] if first else [carried]),
        [(2, 3 * rows, rows)] * 2 if last else [acc_shape],
        [pltpu.VMEM(acc_shape, F32)],
    )


def meet_kernel(first, last, joined, at, far, near, own, cross, basis, y_own, *rest):
    if not first:
        carried, *rest = rest
    if joined:
        old_keep, old_give, *rest = rest
    *outs, core_keep, core_give, acc = rest
    step = pl.program_id(0)
    gy, gz, side = at[0], at[1], at[2]
    base = 0
    if joined:
        base = old_keep.shape[2]

    @pl.when(step == 0)
    def _():
        acc[...] = jnp.zeros_like(acc) if first else carried[...]
        if joined:
            core_keep[:, :, :base] = old_keep[...]
            core_give[:, :, :base] = old_give[...]

    f, n, s, c = far[...], near[...], own[...], cross[...]
    projected = nn(basis[0], n) + nn(basis[1], s) + nn(basis[2], c) + nn(basis[3], f)
    part = nn(projected.astype(BF16), y_own[...])
    acc[0] += nt(f, n)
    acc[1] += nt(f, s)
    acc[2] += nt(f, c)
    few, cols = part.shape[0] // 8, part.shape[1]
    span = pl.ds(pl.multiple_of(base + step * cols, 128), cols)
    for z in range(4):
        k = jnp.where(side == 0, z, 3 - z)
        for out, flag in ((core_keep, gy), (core_give, 1 - gy)):
            for y in range(2):

                @pl.when(flag == y)
                def _(z=z, k=k, y=y, out=out):
                    start = (2 * z + y) * few
                    out[k, :, span] = part[start : start + few]

    @pl.when(step == pl.num_programs(0) - 1)
    def _():
        if not last:
            outs[0][...] = acc[...]
            return
        for k in range(4):
            l = jnp.where(side == 0, k, 3 - k)
            for out, flag in zip(outs, (0, 1)):

                @pl.when(((l & 1) ^ gz) == flag)
                def _(k=k, l=l, out=out):
                    out[(l >> 1) ^ gy] = acc[k] if k < 3 else jnp.zeros_like(acc[0])


def meet(at, far, skip, n, near, own, cross, lo, basis, y_own, carried, old, last):
    rows = far.shape[0]
    ny, s_cols = y_own.shape
    rank = basis.shape[1]
    first, joined = carried is None, old is not None
    shifted = pl.BlockSpec((rows, ny), lambda j, at: (0, lo + j))
    acc_shape = (3, rows, rows)
    core_shape = (4, rank // 8, n * s_cols + (old[0].shape[2] if joined else 0))
    return call(
        "meet",
        functools.partial(meet_kernel, first, last, joined),
        at,
        n,
        [pl.BlockSpec((rows, ny), lambda j, at: (0, skip + j)), shifted, shifted, shifted]
        + [whole(basis.shape), whole(y_own.shape)]
        + ([] if first else [whole(acc_shape)])
        + ([whole(o.shape) for o in old] if joined else []),
        [far, near, own, cross, basis, y_own]
        + ([] if first else [carried])
        + (list(old) if joined else []),
        ([(2, rows, rows)] * 2 if last else [acc_shape]) + [core_shape] * 2,
        [pltpu.VMEM(acc_shape, F32)],
    )


def meeting(snapshot, x_basis, y_basis):
    rows, ncomp, nz, ny = snapshot.shape
    rank = x_basis.shape[1]
    gx, gy, gz = lax.axis_index("gx"), lax.axis_index("gy"), lax.axis_index("gz")
    side = gx // 2
    inner = (gx == 1) | (gx == 2)
    half = ncomp // 2
    width = nz * ny
    inverse = 1.0 / (ncomp * width * lax.axis_size("gy") * lax.axis_size("gz"))
    own_at, oth_at = (1 - side) * half, side * half
    at = jnp.stack([gy, gz, side, inner.astype(jnp.int32)])

    tied = lax.optimization_barrier

    def take(source, start, lo=0, count=rows):
        return lax.dynamic_slice(source, (lo, start, 0, 0), (count, 1, nz, ny)).reshape(count, nz, ny)

    def flat(*parts):
        parts = [a.reshape(a.shape[0], width) for a in parts]
        return parts[0] if len(parts) == 1 else jnp.concatenate(parts, 0)

    near, cross, own, oth = ([None] * half for _ in range(4))
    source = snapshot
    oth_raw, own_raw = [], []
    for lo, count in ((0, rows // 2), (rows // 2, rows - rows // 2)):
        o, w = take(source, oth_at, lo, count), take(source, own_at, lo, count)
        source, o, w = tied((source, o, w))
        oth_raw.append(o)
        own_raw.append(w)
    oth_late = take(source, oth_at + 1)
    source, oth_late = tied((source, oth_late))
    oth[1], own[1] = flat(oth_late), flat(take(source, own_at + 1))
    cross_raw = [lax.ppermute(a, "gx", CROSS) for a in oth_raw]
    near_raw = [lax.ppermute(a, "gx", NEAR) for a in own_raw]
    cross[1] = lax.ppermute(oth[1], "gx", CROSS)
    own[1], cross_raw[0] = tied((own[1], cross_raw[0]))
    near[1] = lax.ppermute(own[1], "gx", NEAR)
    source, oth[1], own[1] = tied((source, oth[1], own[1]))
    oth[0], own[0] = flat(take(source, oth_at)), flat(take(source, own_at))

    places = [
        jnp.where(side == 0, 0, 3),
        gx,
        jnp.where(side == 0, 2, 1),
        jnp.where(side == 0, 3, 0),
    ]
    basis = jnp.stack([lax.dynamic_slice_in_dim(x_basis, p * rows, rows, 0).T for p in places])
    y_own = lax.dynamic_slice_in_dim(y_basis, gy * ny, ny, 0)

    cuts = [(0, 10), (10, 14), (14, 16)]

    def piece(lo, hi):
        parts = []
        for h in range(half):
            a, b = max(lo, h * nz), min(hi, (h + 1) * nz)
            if a < b:
                parts.append(oth[h] if b - a == nz else oth[h][:, (a - h * nz) * ny : (b - h * nz) * ny])
        return parts[0] if len(parts) == 1 else jnp.concatenate(parts, 1)

    def send_far(i, *gate):
        data, gate = tied((sends[i], gate))
        return lax.ppermute(data, "gx", FAR), *gate

    def meets(i, far, carried, old, last=False):
        lo, hi = cuts[i]
        for h in range(half):
            a, b = max(lo, h * nz), min(hi, (h + 1) * nz)
            if a < b:
                carried, *old = meet(
                    at, far, a - lo, b - a, near[h], own[h], cross[h], a - h * nz,
                    basis, y_own, carried, old, False
                ) if not last else wrap_last(meet(
                    at, far, a - lo, b - a, near[h], own[h], cross[h], a - h * nz,
                    basis, y_own, carried, old, True
                ))
        return carried, *old

    def wrap_last(outs):
        return (outs[0], outs[1]), *outs[2:]

    sends = [piece(lo, hi) for lo, hi in cuts]
    sends, cross_raw, own[0] = tied((sends, cross_raw, own[0]))
    top = flat(cross_raw[0])
    top, near_raw[0] = tied((top, near_raw[0]))
    near_top = flat(near_raw[0])
    near_top, cross_raw[1] = tied((near_top, cross_raw[1]))
    cross[0] = jnp.concatenate([top, flat(cross_raw[1])], 0)
    cross[0], near_raw[1] = tied((cross[0], near_raw[1]))
    near[0] = jnp.concatenate([near_top, flat(near_raw[1])], 0)
    far0, cross[0], near[0], own[0], basis, y_own = send_far(
        0, cross[0], near[0], own[0], basis, y_own
    )
    (sums,) = pairs(at, near[0], own[0], cross[0], oth[0], None, False, ny)
    sums, cross[1] = tied((sums, cross[1]))

    far1, cross[1], near[1], sums = send_far(1, cross[1], near[1], sums)
    keep, give = pairs(at, near[1], own[1], cross[1], oth[1], sums, True, ny)

    early, leave = once(
        "add_split", add_split_kernel, at, [keep, lax.ppermute(give, "gz", SWAP)], [keep.shape[1:]] * 2
    )
    got = lax.ppermute(leave, "gy", SWAP)
    far2, far0 = send_far(2, far0)
    far0, got = tied((far0, got))
    acc, *core = meets(0, far0, None, None)
    core_got = lax.ppermute(core[1], "gy", SWAP)
    few, cols = core_got.shape[1:]
    laid = rows + few * len(wrapped(cols, rows))
    home = once(
        "home",
        home_kernel,
        at,
        [early, got, core[0], core_got],
        [(rows, rows), (laid, rows), (few, cols), (laid, rows), (laid - rows, rows)],
        [F32, BF16, F32, BF16, BF16],
    )
    far1, acc, home = tied((far1, acc, home))
    acc, *core = meets(1, far1, acc, None)
    far2, acc, home = tied((far2, acc, home))
    gram_own, near_home, kept_home, cross_home, far_home = home
    (keep, give), *core = meets(2, far2, acc, core, True)

    few, cols = core[0].shape[1:]
    size = few * len(wrapped(cols, rows))
    core_got = lax.ppermute(core[1], "gy", SWAP)
    stay, leave = once(
        "add_late",
        add_late_kernel,
        at,
        [keep, lax.ppermute(give, "gz", SWAP)],
        [(rows, rows)] * 2,
        [F32, BF16],
    )
    full = laid + size
    cross_home = lax.ppermute(cross_home, "gx", CROSS)
    to_near, kept, to_cross = once(
        "join",
        join_kernel,
        at,
        [core[0], core_got, near_home],
        [(full, rows), (few, cols), (size, rows)],
        [BF16, F32, BF16],
    )
    got = lax.ppermute(leave, "gy", SWAP)
    near_got = lax.ppermute(to_near, "gx", NEAR_BACK)
    cross_got = lax.ppermute(to_cross, "gx", CROSS)
    got, cross_home = tied((got, cross_home))
    to_far, turned = once(
        "part",
        part_kernel,
        at,
        [stay, got, core[0], core_got, far_home],
        [(full, rows), (rows, rows)],
        [BF16, BF16],
    )
    return once(
        "final",
        functools.partial(final_kernel, inverse),
        at,
        [
            gram_own,
            kept_home,
            lax.ppermute(to_far, "gx", FAR_BACK),
            lax.ppermute(turned, ("gx", "gy", "gz"), TURN),
            near_got,
            kept,
            cross_home,
            cross_got,
        ],
        [(rows, rows), (few, ncomp, nz, y_basis.shape[1])],
    )


def solution(mesh):
    in_specs = (P(("grp", "gx"), None, "gz", "gy"), P("grp", None), P("grp", None))
    out_specs = (P(("grp", "gx"), ("gy", "gz")), P(("grp", "gx", "gy"), None, "gz", None))
    sizes = (mesh.shape["gx"], mesh.shape["gy"], mesh.shape["gz"])
    body = meeting if sizes == (4, 2, 2) else gathered
    return jax.shard_map(body, mesh=mesh, in_specs=in_specs, out_specs=out_specs, check_vma=False)
```
